32 devices in a mesh: grp: 2 (over x), gy: 16 (over z, y, core).
Axes of the slice: x: 2, y: 2, z: 4, core: 2. Of those that a mesh axis runs over, the one named last changes fastest.
Arguments:
- window_feats: bfloat16 [128, 32, 4, 16, 128], P(('grp', 'gy')), parts along dimension 0, may hold values from -6 to 6
- window_brick: int32 [128], P('grp'), parts along dimension 0, may hold values from 0 to 14, as said below
- window_z: int32 [128], P('grp'), parts along dimension 0, may hold values from 0 to 128, as said below
- window_count: int32 [32], P('grp'), parts along dimension 0, may hold values from 1 to 4, as said below
- gaussian: float32 [4, 16, 128], replicated, may hold values from 0.01 to 400, as said below
- brick_feats: bfloat16 [32, 4, 256, 256], P(None, None, ('grp', 'gy')), parts along dimension 2, may hold values from -85 to 85
- teacher_w1: bfloat16 [32, 32, 3, 3, 3], replicated, may hold values from -0.21875 to 0.21875
- teacher_w2: bfloat16 [16, 32, 3, 3, 3], replicated, may hold values from -0.21875 to 0.21875
- student_w1: bfloat16 [32, 32, 3, 3, 3], replicated, may hold values from -0.21875 to 0.21875
- student_w2: bfloat16 [16, 32, 3, 3, 3], replicated, may hold values from -0.21875 to 0.21875
Outputs:
- teacher_sum: float32 [16, 4, 256, 256], P(None, None, ('grp', 'gy')), parts along dimension 2
- feature_grad: float32 [32, 4, 256, 256], P(None, None, ('grp', 'gy')), parts along dimension 2
The draws below stay inside these ranges and needn't reach their ends.
There are 2 independent parts, one for each index of `grp`. The reference program is written for one: setup_inputs(seed, part) draws one part's arguments, and reference() takes and returns one part's arrays. A program takes and returns all parts, laid end to end along the dimension named above; an argument that names none is the same for every part. Nothing has to cross between parts.
Inputs may be any that keep to these rules, and one draw needn't show every extreme that they name: `window_brick`: slot s names the brick owner s // 4 or the one before it, within 0 to 14. `window_z`: a multiple of 32. `window_count`: some owner has all 4 slots live. `gaussian`: positive.
All inputs are finite; a program needn't handle non-finite values.
Results may differ from the reference program's by a relative error of at most 0.0065.
Values may be sent and summed in bfloat16 or wider, within the bound.
No kernel may reach another device: no remote copies, remote signals or barrier semaphores. Data moves between devices by JAX's collectives and lax.ppermute only.
A program may use at most 128 MiB of HBM per device.

```python
import jax
import jax.numpy as jnp
from jax import lax

C = 32
K = 16
SLOTS = 4
BX = 4
BY = 8
WZ = 128
WINDOWS = 64
N_GY = 16


def draw_window_brick(key, part):
    owner = jnp.arange(SLOTS * N_GY, dtype=jnp.int32) // SLOTS
    step_back = jax.random.randint(key, (SLOTS * N_GY,), 0, 2, dtype=jnp.int32)
    return jnp.clip(owner - step_back, 0, N_GY - 2).astype(jnp.int32)


def draw_window_z(key, part):
    level = jax.random.randint(jax.random.fold_in(key, 5), (SLOTS * N_GY,), 0, 5, dtype=jnp.int32)
    return (level * (WZ // 4)).astype(jnp.int32)


def draw_window_count(key, part):
    heavy = jax.random.randint(jax.random.fold_in(key, 1), (N_GY,), 0, 4, dtype=jnp.int32) == 0
    light = jax.random.randint(jax.random.fold_in(key, 2), (N_GY,), 1, SLOTS // 2 + 1, dtype=jnp.int32)
    counts = jnp.where(heavy, SLOTS, light).astype(jnp.int32)
    busiest = jax.random.randint(jax.random.fold_in(key, 3), (), 0, N_GY, dtype=jnp.int32)
    return counts.at[busiest].set(SLOTS).astype(jnp.int32)


def draw_gaussian(key, part):
    x_pos = (jnp.arange(BX, dtype=jnp.float32) + 0.5) / BX - 0.5
    y_pos = (jnp.arange(2 * BY, dtype=jnp.float32) + 0.5) / (2 * BY) - 0.5
    z_pos = (jnp.arange(WZ, dtype=jnp.float32) + 0.5) / WZ - 0.5
    radius = x_pos[:, None, None] ** 2 + y_pos[None, :, None] ** 2 + z_pos[None, None, :] ** 2
    bump = jnp.exp(-radius / 0.32)
    rough = jax.random.uniform(jax.random.fold_in(key, 7), (BX, 2 * BY, WZ), jnp.float32, 0.5, 1.5)
    return (bump * rough).astype(jnp.float32)


def draw_brick_feats(key, part):
    shape = (C, BX, BY * N_GY, 2 * WZ)
    values = jnp.clip(jax.random.normal(jax.random.fold_in(key, 11), shape, jnp.float32), -6.0, 6.0)
    return values.astype(jnp.bfloat16)


def levels(own_key, dims, pieces, low, top_value):
    def one(dim, blocks):
        heights = jax.random.uniform(jax.random.fold_in(jax.random.fold_in(own_key, 6), dim), (blocks,), jnp.float32, low / len(pieces), top_value / len(pieces))
        return jnp.repeat(jnp.exp(heights), dims[dim] // blocks).reshape((-1,) + (1,) * (len(dims) - dim - 1))

    gain = one(*pieces[0])
    for cut in pieces[1:]:
        gain = gain * one(*cut)
    return gain


def bell_draw(key, extent, scale, most, cuts=(), held_as=jnp.bfloat16):
    array = jax.random.normal(key, extent, jnp.float32) * scale
    if len(cuts) > 0:
        array = levels(key, extent, cuts, -0.22, 0.18) * array
    return jnp.clip(array, min=-most, max=most).astype(held_as)


def setup_inputs(seed: int = 0, part: int = 0) -> dict:
    seeds = jax.random.split(jax.random.key(seed), 11)
    part_splits = jax.random.split(jax.random.fold_in(seeds[10], part), 11)
    window_feats = bell_draw(part_splits[0], (WINDOWS, C, BX, 2 * BY, WZ), 1.0, 6.0, ((0, 16),))
    window_brick = draw_window_brick(jax.random.fold_in(jax.random.fold_in(seeds[10], part), 71), part)
    window_z = draw_window_z(jax.random.fold_in(jax.random.fold_in(seeds[10], part), 71), part)
    window_count = draw_window_count(jax.random.fold_in(jax.random.fold_in(seeds[10], part), 71), part)
    gaussian = draw_gaussian(jax.random.fold_in(seeds[10], 71), part)
    brick_feats = draw_brick_feats(jax.random.fold_in(jax.random.fold_in(seeds[10], part), 71), part)
    teacher_w1 = bell_draw(seeds[6], (C, C, 3, 3, 3), (27 * C) ** -0.5, 0.21875)
    teacher_w2 = bell_draw(seeds[7], (K, C, 3, 3, 3), (27 * C) ** -0.5, 0.21875)
    student_w1 = bell_draw(seeds[8], (C, C, 3, 3, 3), (27 * C) ** -0.5, 0.21875)
    student_w2 = bell_draw(seeds[9], (K, C, 3, 3, 3), (27 * C) ** -0.5, 0.21875)
    return dict(window_feats=window_feats, window_brick=window_brick, window_z=window_z, window_count=window_count, gaussian=gaussian, brick_feats=brick_feats, teacher_w1=teacher_w1, teacher_w2=teacher_w2, student_w1=student_w1, student_w2=student_w2)


def convolve(values, kernel):
    result = lax.conv_general_dilated(values[None].astype(jnp.float32), kernel.astype(jnp.float32), (1, 1, 1), ((1, 1), (1, 1), (1, 1)), dimension_numbers=("NCDHW", "OIDHW", "NCDHW"), precision=lax.Precision.HIGHEST, preferred_element_type=jnp.float32)
    return result[0]


def flipped(kernel):
    return jnp.flip(jnp.transpose(kernel, (1, 0, 2, 3, 4)), axis=(2, 3, 4))


def silu_slope(values):
    sigmoid_value = jax.nn.sigmoid(values)
    return sigmoid_value * (1.0 + values * (1.0 - sigmoid_value))


def reference(window_feats, window_brick, window_z, window_count, gaussian, brick_feats, teacher_w1, teacher_w2, student_w1, student_w2):
    classes = teacher_w2.shape[0]
    slot_total = window_feats.shape[0]
    slot_cap = slot_total // N_GY
    half_rows = gaussian.shape[1] // 2
    start_sum = jnp.zeros((classes, brick_feats.shape[1], brick_feats.shape[2], brick_feats.shape[3]), jnp.float32)

    def add_window(running_sum, inputs):
        window_input, first_brick, z_start, slot_id = inputs
        hidden = jax.nn.silu(convolve(window_input, teacher_w1)).astype(jnp.bfloat16)
        logits = convolve(hidden, teacher_w2)
        live_flag = (slot_id % slot_cap < window_count[slot_id // slot_cap]).astype(jnp.float32)
        weighted = gaussian[None] * logits * live_flag
        start_index = (jnp.int32(0), jnp.int32(0), (first_brick * half_rows).astype(jnp.int32), z_start.astype(jnp.int32))
        current = lax.dynamic_slice(running_sum, start_index, weighted.shape)
        return lax.dynamic_update_slice(running_sum, current + weighted, start_index), None

    teacher_sum = lax.scan(add_window, start_sum, (window_feats, window_brick, window_z, jnp.arange(slot_total, dtype=jnp.int32)))[0]
    targets = jax.nn.softmax(teacher_sum, axis=0)
    student_pre = convolve(brick_feats, student_w1)
    student_hidden = jax.nn.silu(student_pre).astype(jnp.bfloat16)
    student_logits = convolve(student_hidden, student_w2)
    logit_grad = (jax.nn.softmax(student_logits, axis=0) - targets).astype(jnp.bfloat16)
    hidden_grad = convolve(logit_grad, flipped(student_w2))
    pre_grad = (hidden_grad * silu_slope(student_pre)).astype(jnp.bfloat16)
    feature_grad = convolve(pre_grad, flipped(student_w1))
    return (teacher_sum, feature_grad)
```

```python
import functools

import jax
import jax.numpy as jnp
from jax import lax
from jax.experimental import pallas as pl
from jax.experimental.pallas import tpu as pltpu
from jax.sharding import PartitionSpec as P

F32 = jnp.float32
BF16 = jnp.bfloat16
VMEM_BYTES = 56 * 1024 * 1024


def spread(channels, by_x):
    a = lax.broadcasted_iota(jnp.int32, (3, channels, 16 * channels), 0)
    c = lax.broadcasted_iota(jnp.int32, (3, channels, 16 * channels), 1)
    lane = lax.broadcasted_iota(jnp.int32, (3, channels, 16 * channels), 2)
    x = lane // (4 * channels)
    rest = lane % (4 * channels)
    if by_x:
        xi, ci = rest // channels, rest % channels
    else:
        xi, ci = rest % 4, rest // 4
    return ((ci == c) & (xi == x + a - 1)).astype(F32).astype(BF16)


def band(w_ref, hot_ref):
    _, taps, outs, ins = w_ref.shape
    wide = None
    for a in range(3):
        part = jnp.dot(
            w_ref[a].reshape(taps * outs, ins), hot_ref[a], preferred_element_type=F32
        )
        wide = part if wide is None else wide + part
    width = 4 * ins
    result = []
    for t in range(taps):
        rows = wide[t * outs : (t + 1) * outs]
        result.append(
            jnp.concatenate(
                [rows[:, x * width : (x + 1) * width] for x in range(4)], axis=0
            )
        )
    return result


def fill_big(big_ref, blocks, out_rows):
    rows, width = blocks[0].shape
    in_rows = out_rows + 2
    zero = jnp.zeros((rows, width), BF16)
    for yo in range(out_rows):
        for d in range(3):
            for yi in range(in_rows):
                b = yi - yo
                piece = blocks[b * 3 + d].astype(BF16) if 0 <= b < 3 else zero
                col = (d * in_rows + yi) * width
                big_ref[pl.ds(yo * rows, rows), pl.ds(col, width)] = piece


def shifted(v, step):
    lanes = v.shape[-1]
    rolled = pltpu.roll(v, (-step) % lanes, v.ndim - 1)
    lane = lax.broadcasted_iota(jnp.int32, v.shape, v.ndim - 1)
    edge = lane == (lanes - 1 if step > 0 else 0)
    return jnp.where(edge, 0.0, rolled)


def put_row(buf_ref, y, v):
    buf_ref[1, y] = v.astype(BF16)
    buf_ref[0, y] = shifted(v, -1).astype(BF16)
    buf_ref[2, y] = shifted(v, 1).astype(BF16)


def window(buf_ref, y, count):
    rows = buf_ref.shape[2]
    return jnp.concatenate(
        [buf_ref[d, pl.ds(y, count)].reshape(count * rows, -1) for d in range(3)], axis=0
    )


def sigmoid(v):
    return 0.5 + 0.5 * jnp.tanh(0.5 * v)


def teacher_kernel(
    brick_s,
    z_s,
    count_s,
    feats_ref,
    gauss_ref,
    w1_ref,
    w2_ref,
    hot1_ref,
    hot2_ref,
    own_ref,
    pair_ref,
    cross_ref,
    big1,
    big2,
    flat,
    xbuf,
    hbuf,
    total,
):
    slot = pl.program_id(0)
    slots = pl.num_programs(0)
    position = lax.axis_index("gy")
    lanes = 128

    @pl.when(slot == 0)
    def _():
        fill_big(big1, band(w1_ref, hot1_ref), 2)
        fill_big(big2, band(w2_ref, hot2_ref), 4)
        total[...] = jnp.zeros_like(total)
        for y in (0, 17):
            xbuf[:, y] = jnp.zeros((3, 128, lanes), BF16)
            hbuf[:, y] = jnp.zeros((3, 128, lanes), BF16)

    @pl.when(slot < count_s[position])
    def _():
        flat[...] = feats_ref[0].astype(F32)
        for y in range(16):
            put_row(xbuf, y + 1, flat[pl.ds(y, 128, stride=16), :])
        for y in range(0, 8, 2):
            both = jnp.concatenate([window(xbuf, y, 4), window(xbuf, y + 8, 4)], axis=1)
            pre = jnp.dot(big1[...], both, preferred_element_type=F32)
            hid = pre * sigmoid(pre)
            for half in range(2):
                for k in range(2):
                    put_row(
                        hbuf,
                        8 * half + y + k + 1,
                        hid[k * 128 : (k + 1) * 128, half * 128 : (half + 1) * 128],
                    )
        z0 = z_s[position * slots + slot]
        base = 8 * (brick_s[position * slots + slot] - position + 1)
        lane = lax.broadcasted_iota(jnp.int32, (64, lanes), 1)
        first = lane >= z0
        for y in range(0, 8, 4):
            both = jnp.concatenate([window(hbuf, y, 6), window(hbuf, y + 8, 6)], axis=1)
            logits = jnp.dot(big2[...], both, preferred_element_type=F32)
            for half in range(2):
                for k in range(4):
                    row = 8 * half + y + k
                    part = logits[k * 64 : (k + 1) * 64, half * 128 : (half + 1) * 128]
                    weight = jnp.concatenate(
                        [
                            jnp.broadcast_to(gauss_ref[x, row : row + 1, :], (16, lanes))
                            for x in range(4)
                        ],
                        axis=0,
                    )
                    turned = pltpu.roll(part * weight, lax.rem(z0, 128), 1)
                    total[base + row, :, pl.ds(0, 128)] += jnp.where(first, turned, 0.0)
                    total[base + row, :, pl.ds(128, 128)] += jnp.where(first, 0.0, turned)

    @pl.when(slot == slots - 1)
    def _():
        odd = lax.rem(position, 2)
        own_ref[...] = total[8:16]
        pair_ref[...] = total[pl.ds(16 * (1 - odd), 8)]
        cross_ref[...] = total[pl.ds(16 * odd, 8)]


def teacher(brick, z, count, feats, gauss, w1, w2, hot1, hot2):
    slots = feats.shape[0]
    whole = lambda a: pl.BlockSpec(a.shape, lambda s, *_: (0,) * a.ndim)
    sums = jax.ShapeDtypeStruct((8, 64, 256), F32)
    out_spec = pl.BlockSpec((8, 64, 256), lambda s, *_: (0, 0, 0))
    return pl.pallas_call(
        teacher_kernel,
        name="teacher",
        grid_spec=pltpu.PrefetchScalarGridSpec(
            num_scalar_prefetch=3,
            grid=(slots,),
            in_specs=[
                pl.BlockSpec((1, 2048, 128), lambda s, *_: (s, 0, 0)),
                whole(gauss),
                whole(w1),
                whole(w2),
                whole(hot1),
                whole(hot2),
            ],
            out_specs=[out_spec] * 3,
            scratch_shapes=[
                pltpu.VMEM((256, 1536), BF16),
                pltpu.VMEM((256, 2304), BF16),
                pltpu.VMEM((2048, 128), F32),
                pltpu.VMEM((3, 18, 128, 128), BF16),
                pltpu.VMEM((3, 18, 128, 128), BF16),
                pltpu.VMEM((24, 64, 256), F32),
            ],
        ),
        out_shape=[sums] * 3,
        compiler_params=pltpu.CompilerParams(
            dimension_semantics=("arbitrary",), vmem_limit_bytes=VMEM_BYTES
        ),
        cost_estimate=pl.CostEstimate(
            flops=11_000_000_000, bytes_accessed=4_000_000, transcendentals=1_000_000
        ),
    )(brick, z, count, feats, gauss, w1, w2, hot1, hot2)


def relay_kernel(feats_ref, main_ref, pair_ref, cross_ref, flat):
    odd = lax.rem(lax.axis_index("gy"), 2)
    for h in range(2):
        flat[...] = feats_ref[:, pl.ds(h * 128, 128)].astype(F32)
        for y in range(8):
            main_ref[y, :, pl.ds(h * 128, 128)] = flat[pl.ds(y, 128, stride=8), :].astype(BF16)
    pair_ref[...] = main_ref[pl.ds(6 * (1 - odd), 2)]
    cross_ref[...] = main_ref[pl.ds(6 * odd, 2)]


def relay(feats):
    edge = jax.ShapeDtypeStruct((2, 128, 256), BF16)
    return pl.pallas_call(
        relay_kernel,
        name="relay",
        out_shape=[jax.ShapeDtypeStruct((8, 128, 256), BF16), edge, edge],
        scratch_shapes=[pltpu.VMEM((1024, 128), F32)],
        compiler_params=pltpu.CompilerParams(vmem_limit_bytes=VMEM_BYTES),
        cost_estimate=pl.CostEstimate(flops=0, bytes_accessed=1_500_000, transcendentals=0),
    )(feats)


def put_edges(store, pair_ref, cross_ref, low, high):
    odd = lax.rem(lax.axis_index("gy"), 2)
    pair_at = jnp.where(odd == 1, low, high)
    cross_at = jnp.where(odd == 1, high, low)
    for k in range(2):
        store(pair_at + k, pair_ref[k])
        store(cross_at + k, cross_ref[k])


def inside(y):
    position = lax.axis_index("gy")
    last = lax.axis_size("gy") - 1
    if y < 0:
        return jnp.where(position > 0, 1.0, 0.0)
    if y >= 8:
        return jnp.where(position < last, 1.0, 0.0)
    return None


def class_softmax(v):
    parts = []
    for x in range(4):
        block = v[x * 16 : (x + 1) * 16]
        peak = jnp.max(block, axis=0, keepdims=True)
        grown = jnp.exp(block - peak)
        parts.append(grown / jnp.sum(grown, axis=0, keepdims=True))
    return jnp.concatenate(parts, axis=0)


def forward_kernel(
    main_ref,
    pair_ref,
    cross_ref,
    w1_ref,
    w2_ref,
    hot1_ref,
    hot2_ref,
    prob_ref,
    slope_ref,
    big1,
    big2,
    xbuf,
    hbuf,
):
    fill_big(big1, band(w1_ref, hot1_ref), 2)
    fill_big(big2, band(w2_ref, hot2_ref), 4)
    store = lambda y, v: put_row(xbuf, y, v.astype(F32))
    for y in range(8):
        store(y + 2, main_ref[y])
    put_edges(store, pair_ref, cross_ref, 0, 10)
    for y in range(0, 10, 2):
        pre = jnp.dot(big1[...], window(xbuf, y, 4), preferred_element_type=F32)
        sig = sigmoid(pre)
        hid = pre * sig
        slope = sig * (1.0 + pre * (1.0 - sig))
        for k in range(2):
            row = y + k
            rows = slice(k * 128, (k + 1) * 128)
            slope_ref[row] = slope[rows]
            keep = inside(row - 1)
            put_row(hbuf, row, hid[rows] if keep is None else hid[rows] * keep)
    for y in range(0, 8, 4):
        logits = jnp.dot(big2[...], window(hbuf, y, 6), preferred_element_type=F32)
        for k in range(4):
            prob_ref[y + k] = class_softmax(logits[k * 64 : (k + 1) * 64])


def forward(main, pair, cross, w1, w2, hot1, hot2):
    return pl.pallas_call(
        forward_kernel,
        name="forward",
        out_shape=[
            jax.ShapeDtypeStruct((8, 64, 256), F32),
            jax.ShapeDtypeStruct((10, 128, 256), F32),
        ],
        scratch_shapes=[
            pltpu.VMEM((256, 1536), BF16),
            pltpu.VMEM((256, 2304), BF16),
            pltpu.VMEM((3, 12, 128, 256), BF16),
            pltpu.VMEM((3, 10, 128, 256), BF16),
        ],
        compiler_params=pltpu.CompilerParams(vmem_limit_bytes=VMEM_BYTES),
        cost_estimate=pl.CostEstimate(
            flops=4_000_000_000, bytes_accessed=3_000_000, transcendentals=500_000
        ),
    )(main, pair, cross, w1, w2, hot1, hot2)


def combine_kernel(
    own_ref,
    from_pair_ref,
    from_cross_ref,
    prob_ref,
    sum_ref,
    main_ref,
    pair_ref,
    cross_ref,
    turn0,
    turn1,
):
    odd = lax.rem(lax.axis_index("gy"), 2)
    for y in range(8):
        value = own_ref[y] + from_pair_ref[y] + from_cross_ref[y]
        for x in range(4):
            for h, turn in enumerate((turn0, turn1)):
                turn[pl.ds(x * 8 + y, 16, stride=32), :] = value[
                    x * 16 : (x + 1) * 16, h * 128 : (h + 1) * 128
                ]
        main_ref[y] = (prob_ref[y] - class_softmax(value)).astype(BF16)
    pair_ref[...] = main_ref[pl.ds(6 * (1 - odd), 2)]
    cross_ref[...] = main_ref[pl.ds(6 * odd, 2)]
    sum_ref[:, pl.ds(0, 128)] = turn0[...]
    sum_ref[:, pl.ds(128, 128)] = turn1[...]


def combine(own, from_pair, from_cross, prob):
    edge = jax.ShapeDtypeStruct((2, 64, 256), BF16)
    return pl.pallas_call(
        combine_kernel,
        name="combine",
        out_shape=[
            jax.ShapeDtypeStruct((512, 256), F32),
            jax.ShapeDtypeStruct((8, 64, 256), BF16),
            edge,
            edge,
        ],
        scratch_shapes=[pltpu.VMEM((512, 128), F32)] * 2,
        compiler_params=pltpu.CompilerParams(vmem_limit_bytes=VMEM_BYTES),
        cost_estimate=pl.CostEstimate(
            flops=1_000_000, bytes_accessed=3_000_000, transcendentals=200_000
        ),
    )(own, from_pair, from_cross, prob)


def backward_kernel(
    main_ref,
    pair_ref,
    cross_ref,
    slope_ref,
    w1_ref,
    w2_ref,
    hot1_ref,
    hot2_ref,
    out_ref,
    big1,
    big2,
    gbuf,
    pbuf,
    turn0,
    turn1,
):
    flip1 = band(w1_ref, hot1_ref)
    fill_big(big1, [flip1[8 - t].T for t in range(9)], 2)
    flip2 = band(w2_ref, hot2_ref)
    fill_big(big2, [flip2[8 - t].T for t in range(9)], 2)
    store = lambda y, v: put_row(gbuf, y, v.astype(F32))
    for y in range(8):
        store(y + 2, main_ref[y])
    put_edges(store, pair_ref, cross_ref, 0, 10)
    for y in range(0, 10, 2):
        grad = jnp.dot(big2[...], window(gbuf, y, 4), preferred_element_type=F32)
        for k in range(2):
            row = y + k
            pre_grad = grad[k * 128 : (k + 1) * 128] * slope_ref[row]
            keep = inside(row - 1)
            put_row(pbuf, row, pre_grad if keep is None else pre_grad * keep)
    for y in range(0, 8, 2):
        grad = jnp.dot(big1[...], window(pbuf, y, 4), preferred_element_type=F32)
        for k in range(2):
            for x in range(4):
                for h, turn in enumerate((turn0, turn1)):
                    at = k * 128 + x * 32
                    turn[pl.ds(x * 8 + y + k, 32, stride=32), :] = grad[
                        at : at + 32, h * 128 : (h + 1) * 128
                    ]
    out_ref[:, pl.ds(0, 128)] = turn0[...]
    out_ref[:, pl.ds(128, 128)] = turn1[...]


def backward(main, pair, cross, slope, w1, w2, hot1, hot2):
    return pl.pallas_call(
        backward_kernel,
        name="backward",
        out_shape=jax.ShapeDtypeStruct((1024, 256), F32),
        scratch_shapes=[
            pltpu.VMEM((256, 1536), BF16),
            pltpu.VMEM((256, 768), BF16),
            pltpu.VMEM((3, 12, 64, 256), BF16),
            pltpu.VMEM((3, 10, 128, 256), BF16),
            pltpu.VMEM((1024, 128), F32),
            pltpu.VMEM((1024, 128), F32),
        ],
        compiler_params=pltpu.CompilerParams(vmem_limit_bytes=VMEM_BYTES),
        cost_estimate=pl.CostEstimate(
            flops=4_000_000_000, bytes_accessed=3_000_000, transcendentals=0
        ),
    )(main, pair, cross, slope, w1, w2, hot1, hot2)


def swap_pair(value):
    count = lax.axis_size("gy")
    return lax.ppermute(value, "gy", [(i, i ^ 1) for i in range(count)])


def swap_cross(value):
    count = lax.axis_size("gy")
    pairs = [(i, i + 1) for i in range(1, count - 1, 2)]
    return lax.ppermute(value, "gy", pairs + [(j, i) for i, j in pairs])


def taps_first(w):
    outs, ins = w.shape[:2]
    return jnp.transpose(w, (2, 3, 4, 0, 1)).reshape(3, 9, outs, ins)


def body(
    window_feats,
    window_brick,
    window_z,
    window_count,
    gaussian,
    brick_feats,
    teacher_w1,
    teacher_w2,
    student_w1,
    student_w2,
):
    tw1, tw2, sw1, sw2 = map(taps_first, (teacher_w1, teacher_w2, student_w1, student_w2))
    hot_c = spread(32, False)
    hot_x = spread(32, True)
    main, to_pair, to_cross = relay(brick_feats.reshape(1024, 256))
    edge_cross = swap_cross(to_cross)
    edge_pair = swap_pair(to_pair)
    own, sum_pair, sum_cross = teacher(
        window_brick,
        window_z,
        window_count,
        window_feats.reshape(window_feats.shape[0], 2048, 128),
        gaussian,
        tw1,
        tw2,
        hot_c,
        hot_x,
    )
    got_cross = swap_cross(sum_cross)
    got_pair = swap_pair(sum_pair)
    prob, slope = forward(main, edge_pair, edge_cross, sw1, sw2, hot_c, hot_x)
    teacher_sum, grad, grad_pair, grad_cross = combine(own, got_pair, got_cross, prob)
    near_cross = swap_cross(grad_cross)
    near_pair = swap_pair(grad_pair)
    feature_grad = backward(grad, near_pair, near_cross, slope, sw1, sw2, hot_x, hot_x)
    return (teacher_sum.reshape(16, 4, 8, 256), feature_grad.reshape(32, 4, 8, 256))


def solution(mesh):
    placed = (
        P(("grp", "gy"), None, None, None, None),
        P("grp"),
        P("grp"),
        P("grp"),
        P(),
        P(None, None, ("grp", "gy"), None),
        P(),
        P(),
        P(),
        P(),
    )
    return jax.shard_map(
        body,
        mesh=mesh,
        in_specs=placed,
        out_specs=(P(None, None, ("grp", "gy"), None), P(None, None, ("grp", "gy"), None)),
        check_vma=False,
    )
```

```python
import functools

import jax
import jax.numpy as jnp
from jax import lax
from jax.experimental import pallas as pl
from jax.experimental.pallas import tpu as pltpu
from jax.sharding import PartitionSpec as P

F32 = jnp.float32
PITCH = 24
BF16 = jnp.bfloat16
VMEM = pl.BlockSpec(memory_space=pltpu.VMEM)
HBM = pl.BlockSpec(memory_space=pltpu.HBM)


def in_hbm(value):
    return pltpu.with_memory_space_constraint(value, pltpu.HBM)


def params(mib):
    return pltpu.CompilerParams(vmem_limit_bytes=mib * 1024 * 1024)


def cost(flops, moved):
    return pl.CostEstimate(flops=flops, bytes_accessed=moved, transcendentals=0)


def spread(ins, a, by_x):
    c = lax.broadcasted_iota(jnp.int32, (ins, 16 * ins), 0)
    lane = lax.broadcasted_iota(jnp.int32, (ins, 16 * ins), 1)
    x = lane // (4 * ins)
    rest = lane % (4 * ins)
    if by_x:
        xi, ci = rest // ins, rest % ins
    else:
        xi, ci = rest % 4, rest // 4
    return jnp.where((ci == c) & (xi == x + a - 1), 1.0, 0.0).astype(BF16)


def band(w_ref, by_x):
    _, taps, outs, ins = w_ref.shape
    wide = None
    for a in range(3):
        part = jnp.dot(
            w_ref[a].reshape(taps * outs, ins),
            spread(ins, a, by_x),
            preferred_element_type=F32,
        )
        wide = part if wide is None else wide + part
    width = 4 * ins
    result = []
    for t in range(taps):
        rows = wide[t * outs : (t + 1) * outs]
        result.append(
            jnp.concatenate(
                [rows[:, x * width : (x + 1) * width] for x in range(4)], axis=0
            )
        )
    return result


def fill_big(big_ref, blocks, out_rows):
    rows, width = blocks[0].shape
    in_rows = out_rows + 2
    zero = jnp.zeros((rows, width), BF16)
    for yo in range(out_rows):
        for d in range(3):
            for yi in range(in_rows):
                b = yi - yo
                piece = blocks[b * 3 + d].astype(BF16) if 0 <= b < 3 else zero
                col = (d * in_rows + yi) * width
                big_ref[pl.ds(yo * rows, rows), pl.ds(col, width)] = piece


def shifted(v, step):
    lanes = v.shape[-1]
    rolled = pltpu.roll(v, (-step) % lanes, v.ndim - 1)
    lane = lax.broadcasted_iota(jnp.int32, v.shape, v.ndim - 1)
    edge = lane == (lanes - 1 if step > 0 else 0)
    return jnp.where(edge, 0.0, rolled)


def put_row(buf_ref, y, v, lane=0):
    lanes = pl.ds(lane, v.shape[-1])
    buf_ref[1, y, :, lanes] = v.astype(BF16)
    buf_ref[0, y, :, lanes] = shifted(v, -1).astype(BF16)
    buf_ref[2, y, :, lanes] = shifted(v, 1).astype(BF16)


def window(buf_ref, y, count):
    rows = buf_ref.shape[2]
    return jnp.concatenate(
        [buf_ref[d, pl.ds(y, count)].reshape(count * rows, -1) for d in range(3)], axis=0
    )


def sigmoid(v):
    return 0.5 + 0.5 * jnp.tanh(0.5 * v)


def parity():
    return lax.rem(lax.axis_index("gy"), 2)


def teacher_half(
    own, tables, ready, feats_ref, gauss_ref, big1, big2, store, flat, xbuf, hbuf
):
    brick_s, z_s, count_s = tables
    position = lax.axis_index("gy")
    slots = feats_ref.shape[0]
    lanes = 128
    count = count_s[position]
    lane = lax.broadcasted_iota(jnp.int32, (64, lanes), 1)
    z0, mine, base = [], [], []
    for s in range(slots):
        slot = position * slots + s
        z0.append(z_s[slot])
        mine.append(brick_s[slot] == position)
        base.append(jnp.where(mine[s], 0, 8) if own else jnp.where(mine[s], 8, 0))
    low_end = [jnp.where(base[s] == 0, 0.0, 1.0) for s in range(slots)]
    high_end = [jnp.where(base[s] == 8, 0.0, 1.0) for s in range(slots)]
    emitted = set()
    value = {}

    def unpack(s):
        if ("u", s) not in emitted:
            emitted.add(("u", s))
            ready(s)
            flat[s, :, pl.ds(0, 16)] = feats_ref[s].astype(F32).reshape(128, 16, 128)

    def x_row(duo, q):
        if ("x", duo, q) in emitted:
            return
        emitted.add(("x", duo, q))
        for k in range(2):
            s = 2 * duo + k
            unpack(s)
            row = jnp.clip(base[s] - 2 + q, 0, 15)
            v = flat.at[s].reshape(128 * PITCH, 128)[pl.ds(row, 128, stride=PITCH), :]
            if q < 2:
                v = v * low_end[s]
            if q > 9:
                v = v * high_end[s]
            put_row(xbuf.at[duo], q, v, k * lanes)

    def before(op):
        kind, duo, q = op
        if kind == "hidden":
            for r in range(q, q + 4):
                x_row(duo, r)

    def product(op):
        kind, duo, q = op
        if kind == "hidden":
            big, data = big1, window(xbuf.at[duo], q, 4)
        else:
            big, data = big2, window(hbuf.at[duo], q, 4)
        value[op] = jnp.dot(big[...], data, preferred_element_type=F32)

    def after(op):
        kind, duo, q = op
        out = value.pop(op)
        if kind == "hidden":
            hid = out * sigmoid(out)
            for r in range(2):
                for k in range(2):
                    v = hid[r * 128 : (r + 1) * 128, k * lanes : (k + 1) * lanes]
                    if q + r == 0:
                        v = v * low_end[2 * duo + k]
                    if q + r == 9:
                        v = v * high_end[2 * duo + k]
                    put_row(hbuf.at[duo], q + r, v, k * lanes)
            return
        for k in range(2):
            s = 2 * duo + k
            live = jnp.where(s < count, 1.0, 0.0)
            keep = lane >= z0[s]
            for r in range(2):
                part = out[r * 64 : (r + 1) * 64, k * lanes : (k + 1) * lanes]
                weight = jnp.concatenate(
                    [
                        jnp.broadcast_to(
                            gauss_ref[x, pl.ds(base[s] + q + r, 1), :] * live, (16, lanes)
                        )
                        for x in range(4)
                    ],
                    axis=0,
                )
                turned = pltpu.roll(part * weight, lax.rem(z0[s], 128), 1)
                store(mine[s], q + r, jnp.where(keep, turned, 0.0), jnp.where(keep, 0.0, turned))

    order = []
    late = []
    for duo in range(slots // 2):
        for q in range(0, 10, 2):
            order.append(("hidden", duo, q))
            if late:
                order.append(late.pop(0))
        late = [("logits", duo, q) for q in range(0, 8, 2)]
    order += late
    before(order[0])
    before(order[1])
    for i, op in enumerate(order):
        product(op)
        if i > 0:
            after(order[i - 1])
        if i + 2 < len(order):
            before(order[i + 2])
    after(order[-1])


def outer_kernel(
    brick_s,
    z_s,
    count_s,
    feats_hbm,
    gauss_hbm,
    w1_hbm,
    w2_hbm,
    relayed,
    pair_ref,
    cross_ref,
    big1,
    big2,
    feats_ref,
    gauss_ref,
    w1_ref,
    w2_ref,
    flat,
    xbuf,
    hbuf,
    total,
    sems,
):
    slots = feats_ref.shape[0]
    copies = [
        pltpu.make_async_copy(w1_hbm, w1_ref, sems.at[slots]),
        pltpu.make_async_copy(w2_hbm, w2_ref, sems.at[slots + 1]),
        pltpu.make_async_copy(gauss_hbm, gauss_ref, sems.at[slots + 2]),
    ]
    for copy in copies:
        copy.start()
    loads = [
        pltpu.make_async_copy(feats_hbm.at[s], feats_ref.at[s], sems.at[s]) for s in range(slots)
    ]
    for load in loads:
        load.start()
    total[...] = jnp.zeros_like(total)
    for copy in copies:
        copy.wait()
    fill_big(big1, band(w1_ref, False), 2)
    fill_big(big2, band(w2_ref, True), 2)
    for load in loads:
        load.wait()

    def store(mine, row, low, high):
        side = jnp.where(mine, 1, 0)
        total[side, row, :, pl.ds(0, 128)] += low
        total[side, row, :, pl.ds(128, 128)] += high

    teacher_half(
        False,
        (brick_s, z_s, count_s),
        lambda s: None,
        feats_ref,
        gauss_ref,
        big1,
        big2,
        store,
        flat,
        xbuf,
        hbuf,
    )
    odd = parity()
    pair_ref[...] = total[1 - odd]
    cross_ref[...] = total[odd]


def own_kernel(
    brick_s,
    z_s,
    count_s,
    feats_ref,
    gauss_ref,
    big1,
    big2,
    pair_edge,
    cross_edge,
    own_ref,
    flat,
    xbuf,
    hbuf,
):
    own_ref[...] = jnp.zeros_like(own_ref)

    def store(mine, row, low, high):
        own_ref[row, :, pl.ds(0, 128)] += low
        own_ref[row, :, pl.ds(128, 128)] += high

    teacher_half(
        True,
        (brick_s, z_s, count_s),
        lambda s: None,
        feats_ref,
        gauss_ref,
        big1,
        big2,
        store,
        flat,
        xbuf,
        hbuf,
    )


SUMS = jax.ShapeDtypeStruct((8, 64, 256), F32)


def teacher_scratch(slots):
    return [
        pltpu.VMEM((slots, 128, PITCH, 128), F32),
        pltpu.VMEM((slots // 2, 3, 12, 128, 256), BF16),
        pltpu.VMEM((slots // 2, 3, 10, 128, 256), BF16),
    ]


def teacher_outer(brick, z, count, feats, gauss, w1, w2, relayed):
    slots = feats.shape[0]
    return pl.pallas_call(
        outer_kernel,
        name="teacher_outer",
        grid_spec=pltpu.PrefetchScalarGridSpec(
            num_scalar_prefetch=3,
            in_specs=[HBM] * 4 + [VMEM],
            out_specs=[VMEM] * 6,
            scratch_shapes=[pltpu.VMEM(w1.shape, BF16), pltpu.VMEM(w2.shape, BF16)]
            + teacher_scratch(slots)
            + [pltpu.VMEM((2, 8, 64, 256), F32), pltpu.SemaphoreType.DMA((slots + 3,))],
        ),
        out_shape=[
            SUMS,
            SUMS,
            jax.ShapeDtypeStruct((256, 1536), BF16),
            jax.ShapeDtypeStruct((128, 1536), BF16),
            jax.ShapeDtypeStruct(feats.shape, BF16),
            jax.ShapeDtypeStruct(gauss.shape, F32),
        ],
        compiler_params=params(28),
        cost_estimate=cost(5_000_000_000, 4_000_000),
    )(*map(in_hbm, (brick, z, count, feats, gauss, w1, w2)), relayed)


def teacher_own(brick, z, count, feats, gauss, big1, big2, pair, cross):
    return pl.pallas_call(
        own_kernel,
        name="teacher_own",
        grid_spec=pltpu.PrefetchScalarGridSpec(
            num_scalar_prefetch=3,
            in_specs=[VMEM] * 6,
            out_specs=VMEM,
            scratch_shapes=teacher_scratch(feats.shape[0]),
        ),
        out_shape=SUMS,
        compiler_params=params(28),
        cost_estimate=cost(4_000_000_000, 3_000_000),
    )(*map(in_hbm, (brick, z, count)), feats, gauss, big1, big2, pair, cross)


def relay_kernel(feats_hbm, main_ref, pair_ref, cross_ref, feats_ref, flat, sems):
    odd = parity()
    chunks = 4
    rows = 1024 // chunks
    loads = []
    for i in range(chunks):
        part = pl.ds(i * rows, rows)
        loads.append(pltpu.make_async_copy(feats_hbm.at[part], feats_ref.at[part], sems.at[i]))
        loads[i].start()
    for i in range(chunks):
        loads[i].wait()
        part = pl.ds(i * rows, rows)
        for h in range(2):
            flat[h, part] = feats_ref[part, pl.ds(h * 128, 128)].astype(F32)
            for y in range(8):
                main_ref[y, pl.ds(i * rows // 8, rows // 8), pl.ds(h * 128, 128)] = flat[
                    h, pl.ds(i * rows + y, rows // 8, stride=8), :
                ].astype(BF16)
    pair_ref[...] = main_ref[pl.ds(6 * (1 - odd), 2)]
    cross_ref[...] = main_ref[pl.ds(6 * odd, 2)]


def relay(feats):
    edge = jax.ShapeDtypeStruct((2, 128, 256), BF16)
    return pl.pallas_call(
        relay_kernel,
        name="relay",
        in_specs=[HBM],
        out_specs=[VMEM] * 3,
        out_shape=[jax.ShapeDtypeStruct((8, 128, 256), BF16), edge, edge],
        scratch_shapes=[
            pltpu.VMEM((1024, 256), BF16),
            pltpu.VMEM((2, 1024, 128), F32),
            pltpu.SemaphoreType.DMA((4,)),
        ],
        compiler_params=params(8),
        cost_estimate=cost(0, 1_500_000),
    )(in_hbm(feats))


def put_edges(store, pair_ref, cross_ref, low, high):
    odd = parity()
    for k in range(2):
        pair, cross = pair_ref[k].astype(F32), cross_ref[k].astype(F32)
        store(low + k, jnp.where(odd == 1, pair, cross))
        store(high + k, jnp.where(odd == 1, cross, pair))


def inside(y):
    position = lax.axis_index("gy")
    last = lax.axis_size("gy") - 1
    if y < 0:
        return jnp.where(position > 0, 1.0, 0.0)
    if y >= 8:
        return jnp.where(position < last, 1.0, 0.0)
    return None


def class_softmax(v):
    parts = []
    for x in range(4):
        block = v[x * 16 : (x + 1) * 16]
        peak = jnp.max(block, axis=0, keepdims=True)
        grown = jnp.exp(block - peak)
        parts.append(grown * (1.0 / jnp.sum(grown, axis=0, keepdims=True)))
    return jnp.concatenate(parts, axis=0)


def forward_kernel(
    main_ref, pair_ref, cross_ref, w1_ref, w2_ref, prob_ref, slope_ref, big1, big2, xbuf, hbuf
):
    fill_big(big1, band(w1_ref, False), 2)
    fill_big(big2, band(w2_ref, True), 2)
    store = lambda y, v: put_row(xbuf, y, v)
    put_edges(store, pair_ref, cross_ref, 0, 10)
    for y in range(2):
        store(y + 2, main_ref[y].astype(F32))
    for y in range(0, 10, 2):
        pre = jnp.dot(big1[...], window(xbuf, y, 4), preferred_element_type=F32)
        if y < 6:
            for k in range(2):
                store(y + k + 4, main_ref[y + k + 2].astype(F32))
        sig = sigmoid(pre)
        hid = pre * sig
        slope = sig * (1.0 + pre * (1.0 - sig))
        for k in range(2):
            row = y + k
            rows = slice(k * 128, (k + 1) * 128)
            slope_ref[row] = slope[rows]
            keep = inside(row - 1)
            put_row(hbuf, row, hid[rows] if keep is None else hid[rows] * keep)
    for y in range(0, 8, 2):
        logits = jnp.dot(big2[...], window(hbuf, y, 4), preferred_element_type=F32)
        for k in range(2):
            prob_ref[y + k] = class_softmax(logits[k * 64 : (k + 1) * 64])


def forward(main, pair, cross, w1, w2):
    return pl.pallas_call(
        forward_kernel,
        name="forward",
        in_specs=[VMEM] * 5,
        out_specs=[VMEM] * 2,
        out_shape=[SUMS, jax.ShapeDtypeStruct((10, 128, 256), F32)],
        scratch_shapes=[
            pltpu.VMEM((256, 1536), BF16),
            pltpu.VMEM((128, 1536), BF16),
            pltpu.VMEM((3, 12, 128, 256), BF16),
            pltpu.VMEM((3, 10, 128, 256), BF16),
        ],
        compiler_params=params(24),
        cost_estimate=cost(4_000_000_000, 3_000_000),
    )(main, pair, cross, w1, w2)


def combine_kernel(
    own_ref,
    from_pair_ref,
    from_cross_ref,
    prob_ref,
    sum_ref,
    main_ref,
    pair_ref,
    cross_ref,
    turn0,
    turn1,
):
    odd = parity()
    for y in range(8):
        value = own_ref[y] + from_pair_ref[y] + from_cross_ref[y]
        for x in range(4):
            for h, turn in enumerate((turn0, turn1)):
                turn[pl.ds(x * 8 + y, 16, stride=32), :] = value[
                    x * 16 : (x + 1) * 16, h * 128 : (h + 1) * 128
                ]
        main_ref[y] = (prob_ref[y] - class_softmax(value)).astype(BF16)
    pair_ref[...] = main_ref[pl.ds(6 * (1 - odd), 2)]
    cross_ref[...] = main_ref[pl.ds(6 * odd, 2)]
    sum_ref[:, pl.ds(0, 128)] = turn0[...]
    sum_ref[:, pl.ds(128, 128)] = turn1[...]


def combine(own, from_pair, from_cross, prob):
    edge = jax.ShapeDtypeStruct((2, 64, 256), BF16)
    return pl.pallas_call(
        combine_kernel,
        name="combine",
        in_specs=[VMEM] * 4,
        out_specs=[VMEM] * 4,
        out_shape=[
            jax.ShapeDtypeStruct((512, 256), F32),
            jax.ShapeDtypeStruct((8, 64, 256), BF16),
            edge,
            edge,
        ],
        scratch_shapes=[pltpu.VMEM((512, 128), F32)] * 2,
        compiler_params=params(8),
        cost_estimate=cost(1_000_000, 3_000_000),
    )(own, from_pair, from_cross, prob)


def put_out(turns, y, grad):
    for k in range(2):
        for x in range(4):
            for h, turn in enumerate(turns):
                at = k * 128 + x * 32
                turn[pl.ds(x * 8 + y + k, 32, stride=32), :] = grad[
                    at : at + 32, h * 128 : (h + 1) * 128
                ]


def inner_kernel(main_ref, slope_ref, w1_ref, w2_ref, turn0, turn1, pbuf, big1, big2, gbuf):
    flip2 = band(w2_ref, True)
    fill_big(big2, [flip2[8 - t].T for t in range(9)], 2)
    flip1 = band(w1_ref, True)
    fill_big(big1, [flip1[8 - t].T for t in range(9)], 2)
    for y in range(8):
        put_row(gbuf, y, main_ref[y].astype(F32))
    for y in range(0, 6, 2):
        grad = jnp.dot(big2[...], window(gbuf, y, 4), preferred_element_type=F32)
        for k in range(2):
            put_row(pbuf, y + k, grad[k * 128 : (k + 1) * 128] * slope_ref[y + k + 2])
    for y in range(0, 4, 2):
        grad = jnp.dot(big1[...], window(pbuf, y, 4), preferred_element_type=F32)
        put_out((turn0, turn1), y + 2, grad)


def inner(main, slope, w1, w2):
    turned = jax.ShapeDtypeStruct((1024, 128), F32)
    return pl.pallas_call(
        inner_kernel,
        name="inner",
        in_specs=[VMEM] * 4,
        out_specs=[VMEM] * 5,
        out_shape=[
            turned,
            turned,
            jax.ShapeDtypeStruct((3, 6, 128, 256), BF16),
            jax.ShapeDtypeStruct((256, 1536), BF16),
            jax.ShapeDtypeStruct((256, 768), BF16),
        ],
        scratch_shapes=[pltpu.VMEM((3, 8, 64, 256), BF16)],
        compiler_params=params(16),
        cost_estimate=cost(2_000_000_000, 3_000_000),
    )(main, slope, w1, w2)


def outer_rows_kernel(
    main_ref,
    pair_ref,
    cross_ref,
    slope_ref,
    done0,
    done1,
    pin_ref,
    big1,
    big2,
    out_ref,
    gbuf,
    pbuf,
    turn0,
    turn1,
):
    store = lambda y, v: put_row(gbuf, y, v)
    put_edges(store, pair_ref, cross_ref, 0, 6)
    for y, row in ((2, 0), (3, 1), (4, 6), (5, 7)):
        store(y, main_ref[row].astype(F32))
    for d in range(3):
        pbuf[d, pl.ds(2, 2)] = pin_ref[d, pl.ds(0, 2)]
        pbuf[d, pl.ds(4, 2)] = pin_ref[d, pl.ds(4, 2)]
    for g, p, row in ((0, 0, -1), (4, 6, 7)):
        grad = jnp.dot(big2[...], window(gbuf, g, 4), preferred_element_type=F32)
        for k in range(2):
            v = grad[k * 128 : (k + 1) * 128] * slope_ref[row + k + 1]
            keep = inside(row + k)
            put_row(pbuf, p + k, v if keep is None else v * keep)
    for p, row in ((0, 0), (4, 6)):
        grad = jnp.dot(big1[...], window(pbuf, p, 4), preferred_element_type=F32)
        put_out((turn0, turn1), row, grad)
    y = lax.broadcasted_iota(jnp.int32, (1024, 128), 0) % 8
    early = (y >= 2) & (y < 6)
    out_ref[:, pl.ds(0, 128)] = jnp.where(early, done0[...], turn0[...])
    out_ref[:, pl.ds(128, 128)] = jnp.where(early, done1[...], turn1[...])


def outer_rows(main, pair, cross, slope, done0, done1, pin, big1, big2):
    return pl.pallas_call(
        outer_rows_kernel,
        name="outer_rows",
        in_specs=[VMEM] * 9,
        out_specs=VMEM,
        out_shape=jax.ShapeDtypeStruct((1024, 256), F32),
        scratch_shapes=[
            pltpu.VMEM((3, 8, 64, 256), BF16),
            pltpu.VMEM((3, 8, 128, 256), BF16),
            pltpu.VMEM((1024, 128), F32),
            pltpu.VMEM((1024, 128), F32),
        ],
        compiler_params=params(16),
        cost_estimate=cost(2_000_000_000, 3_000_000),
    )(main, pair, cross, slope, done0, done1, pin, big1, big2)


def swap_pair(value):
    count = lax.axis_size("gy")
    return lax.ppermute(value, "gy", [(i, i ^ 1) for i in range(count)])


def swap_cross(value):
    count = lax.axis_size("gy")
    pairs = [(i, i + 1) for i in range(1, count - 1, 2)]
    return lax.ppermute(value, "gy", pairs + [(j, i) for i, j in pairs])


def taps_first(w):
    outs, ins = w.shape[:2]
    return jnp.transpose(w, (2, 3, 4, 0, 1)).reshape(3, 9, outs, ins)


def body(
    window_feats,
    window_brick,
    window_z,
    window_count,
    gaussian,
    brick_feats,
    teacher_w1,
    teacher_w2,
    student_w1,
    student_w2,
):
    tw1, tw2, sw1, sw2 = map(taps_first, (teacher_w1, teacher_w2, student_w1, student_w2))
    main, to_pair, to_cross = relay(brick_feats.reshape(1024, 256))
    edge_cross = swap_cross(to_cross)
    edge_pair = swap_pair(to_pair)
    feats = window_feats.reshape(window_feats.shape[0], 2048, 128)
    tables = (window_brick, window_z, window_count)
    sum_pair, sum_cross, *kept = teacher_outer(*tables, feats, gaussian, tw1, tw2, to_pair)
    got_cross = swap_cross(sum_cross)
    got_pair = swap_pair(sum_pair)
    big1, big2, held_feats, held_gauss = kept
    own = teacher_own(*tables, held_feats, held_gauss, big1, big2, edge_pair, edge_cross)
    prob, slope = forward(main, edge_pair, edge_cross, sw1, sw2)
    teacher_sum, grad, grad_pair, grad_cross = combine(own, got_pair, got_cross, prob)
    near_cross = swap_cross(grad_cross)
    near_pair = swap_pair(grad_pair)
    early = inner(grad, slope, sw1, sw2)
    feature_grad = outer_rows(grad, near_pair, near_cross, slope, *early)
    return (teacher_sum.reshape(16, 4, 8, 256), feature_grad.reshape(32, 4, 8, 256))


def solution(mesh):
    placed = (
        P(("grp", "gy"), None, None, None, None),
        P("grp"),
        P("grp"),
        P("grp"),
        P(),
        P(None, None, ("grp", "gy"), None),
        P(),
        P(),
        P(),
        P(),
    )
    return jax.shard_map(
        body,
        mesh=mesh,
        in_specs=placed,
        out_specs=(P(None, None, ("grp", "gy"), None), P(None, None, ("grp", "gy"), None)),
        check_vma=False,
    )
```

```python
import functools

import jax
import jax.numpy as jnp
from jax import lax
from jax.experimental import pallas as pl
from jax.experimental.pallas import tpu as pltpu
from jax.sharding import PartitionSpec as P

F32 = jnp.float32
PITCH = 24
BF16 = jnp.bfloat16
VMEM = pl.BlockSpec(memory_space=pltpu.VMEM)
HBM = pl.BlockSpec(memory_space=pltpu.HBM)


def in_hbm(value):
    return pltpu.with_memory_space_constraint(value, pltpu.HBM)


def params(mib):
    return pltpu.CompilerParams(vmem_limit_bytes=mib * 1024 * 1024)


def cost(flops, moved):
    return pl.CostEstimate(flops=flops, bytes_accessed=moved, transcendentals=0)


def spread(ins, a, by_x):
    c = lax.broadcasted_iota(jnp.int32, (ins, 16 * ins), 0)
    lane = lax.broadcasted_iota(jnp.int32, (ins, 16 * ins), 1)
    x = lane // (4 * ins)
    rest = lane % (4 * ins)
    if by_x:
        xi, ci = rest // ins, rest % ins
    else:
        xi, ci = rest % 4, rest // 4
    return jnp.where((ci == c) & (xi == x + a - 1), 1.0, 0.0).astype(BF16)


def band(w_ref, by_x):
    _, taps, outs, ins = w_ref.shape
    wide = None
    for a in range(3):
        part = jnp.dot(
            w_ref[a].reshape(taps * outs, ins),
            spread(ins, a, by_x),
            preferred_element_type=F32,
        )
        wide = part if wide is None else wide + part
    width = 4 * ins
    result = []
    for t in range(taps):
        rows = wide[t * outs : (t + 1) * outs]
        result.append(
            jnp.concatenate(
                [rows[:, x * width : (x + 1) * width] for x in range(4)], axis=0
            )
        )
    return result


def fill_big(big_ref, blocks, out_rows):
    rows, width = blocks[0].shape
    in_rows = out_rows + 2
    zero = jnp.zeros((rows, width), BF16)
    for yo in range(out_rows):
        for d in range(3):
            for yi in range(in_rows):
                b = yi - yo
                piece = blocks[b * 3 + d].astype(BF16) if 0 <= b < 3 else zero
                col = (d * in_rows + yi) * width
                big_ref[pl.ds(yo * rows, rows), pl.ds(col, width)] = piece


def shifted(v, step):
    lanes = v.shape[-1]
    rolled = pltpu.roll(v, (-step) % lanes, v.ndim - 1)
    lane = lax.broadcasted_iota(jnp.int32, v.shape, v.ndim - 1)
    edge = lane == (lanes - 1 if step > 0 else 0)
    return jnp.where(edge, 0.0, rolled)


def put_row(buf_ref, y, v, lane=0):
    lanes = pl.ds(lane, v.shape[-1])
    buf_ref[1, y, :, lanes] = v.astype(BF16)
    buf_ref[0, y, :, lanes] = shifted(v, -1).astype(BF16)
    buf_ref[2, y, :, lanes] = shifted(v, 1).astype(BF16)


def window(buf_ref, y, count):
    rows = buf_ref.shape[2]
    return jnp.concatenate(
        [buf_ref[d, pl.ds(y, count)].reshape(count * rows, -1) for d in range(3)], axis=0
    )


def sigmoid(v):
    return 0.5 + 0.5 * jnp.tanh(0.5 * v)


def parity():
    return lax.rem(lax.axis_index("gy"), 2)


def teacher_half(
    own, tables, ready, feats_ref, gauss_ref, big1, big2, store, flat, xbuf, hbuf
):
    brick_s, z_s, count_s = tables
    position = lax.axis_index("gy")
    slots = feats_ref.shape[0]
    lanes = 128
    count = count_s[position]
    lane = lax.broadcasted_iota(jnp.int32, (64, lanes), 1)
    z0, mine, base = [], [], []
    for s in range(slots):
        slot = position * slots + s
        z0.append(z_s[slot])
        mine.append(brick_s[slot] == position)
        base.append(jnp.where(mine[s], 0, 8) if own else jnp.where(mine[s], 8, 0))
    low_end = [jnp.where(base[s] == 0, 0.0, 1.0) for s in range(slots)]
    high_end = [jnp.where(base[s] == 8, 0.0, 1.0) for s in range(slots)]
    emitted = set()
    value = {}

    def unpack(s):
        if ("u", s) not in emitted:
            emitted.add(("u", s))
            ready(s)
            flat[s, :, pl.ds(0, 16)] = feats_ref[s].astype(F32).reshape(128, 16, 128)

    def x_row(duo, q):
        if ("x", duo, q) in emitted:
            return
        emitted.add(("x", duo, q))
        for k in range(2):
            s = 2 * duo + k
            unpack(s)
            row = jnp.clip(base[s] - 2 + q, 0, 15)
            v = flat.at[s].reshape(128 * PITCH, 128)[pl.ds(row, 128, stride=PITCH), :]
            if q < 2:
                v = v * low_end[s]
            if q > 9:
                v = v * high_end[s]
            put_row(xbuf.at[duo], q, v, k * lanes)

    def before(op):
        kind, duo, q = op
        if kind == "hidden":
            for r in range(q, q + 4):
                x_row(duo, r)

    def product(op):
        kind, duo, q = op
        if kind == "hidden":
            big, data = big1, window(xbuf.at[duo], q, 4)
        else:
            big, data = big2, window(hbuf.at[duo], q, 4)
        value[op] = jnp.dot(big[...], data, preferred_element_type=F32)

    def after(op):
        kind, duo, q = op
        out = value.pop(op)
        if kind == "hidden":
            hid = out * sigmoid(out)
            for r in range(2):
                for k in range(2):
                    v = hid[r * 128 : (r + 1) * 128, k * lanes : (k + 1) * lanes]
                    if q + r == 0:
                        v = v * low_end[2 * duo + k]
                    if q + r == 9:
                        v = v * high_end[2 * duo + k]
                    put_row(hbuf.at[duo], q + r, v, k * lanes)
            return
        for k in range(2):
            s = 2 * duo + k
            live = jnp.where(s < count, 1.0, 0.0)
            keep = lane >= z0[s]
            for r in range(2):
                part = out[r * 64 : (r + 1) * 64, k * lanes : (k + 1) * lanes]
                weight = jnp.concatenate(
                    [
                        jnp.broadcast_to(
                            gauss_ref[x, pl.ds(base[s] + q + r, 1), :] * live, (16, lanes)
                        )
                        for x in range(4)
                    ],
                    axis=0,
                )
                turned = pltpu.roll(part * weight, lax.rem(z0[s], 128), 1)
                store(mine[s], q + r, jnp.where(keep, turned, 0.0), jnp.where(keep, 0.0, turned))

    order = []
    late = []
    for duo in range(slots // 2):
        for q in range(0, 10, 2):
            order.append(("hidden", duo, q))
            if late:
                order.append(late.pop(0))
        late = [("logits", duo, q) for q in range(0, 8, 2)]
    order += late
    before(order[0])
    before(order[1])
    for i, op in enumerate(order):
        product(op)
        if i > 0:
            after(order[i - 1])
        if i + 2 < len(order):
            before(order[i + 2])
    after(order[-1])


def outer_kernel(
    brick_s,
    z_s,
    count_s,
    feats_hbm,
    gauss_hbm,
    w1_hbm,
    w2_hbm,
    pair_ref,
    cross_ref,
    big1,
    big2,
    feats_ref,
    gauss_ref,
    w1_ref,
    w2_ref,
    flat,
    xbuf,
    hbuf,
    total,
    sems,
):
    slots = feats_ref.shape[0]
    copies = [
        pltpu.make_async_copy(w1_hbm, w1_ref, sems.at[slots]),
        pltpu.make_async_copy(w2_hbm, w2_ref, sems.at[slots + 1]),
        pltpu.make_async_copy(gauss_hbm, gauss_ref, sems.at[slots + 2]),
    ]
    for copy in copies:
        copy.start()
    loads = [
        pltpu.make_async_copy(feats_hbm.at[s], feats_ref.at[s], sems.at[s]) for s in range(slots)
    ]
    for load in loads:
        load.start()
    total[...] = jnp.zeros_like(total)
    for copy in copies:
        copy.wait()
    fill_big(big1, band(w1_ref, False), 2)
    fill_big(big2, band(w2_ref, True), 2)

    def store(mine, row, low, high):
        side = jnp.where(mine, 1, 0)
        total[side, row, :, pl.ds(0, 128)] += low
        total[side, row, :, pl.ds(128, 128)] += high

    teacher_half(
        False,
        (brick_s, z_s, count_s),
        lambda s: loads[s].wait(),
        feats_ref,
        gauss_ref,
        big1,
        big2,
        store,
        flat,
        xbuf,
        hbuf,
    )
    odd = parity()
    pair_ref[...] = total[1 - odd]
    cross_ref[...] = total[odd]


def own_kernel(
    brick_s,
    z_s,
    count_s,
    feats_ref,
    gauss_ref,
    big1,
    big2,
    own_ref,
    flat,
    xbuf,
    hbuf,
):
    own_ref[...] = jnp.zeros_like(own_ref)

    def store(mine, row, low, high):
        own_ref[row, :, pl.ds(0, 128)] += low
        own_ref[row, :, pl.ds(128, 128)] += high

    teacher_half(
        True,
        (brick_s, z_s, count_s),
        lambda s: None,
        feats_ref,
        gauss_ref,
        big1,
        big2,
        store,
        flat,
        xbuf,
        hbuf,
    )


SUMS = jax.ShapeDtypeStruct((8, 64, 256), F32)


def teacher_scratch(slots):
    return [
        pltpu.VMEM((slots, 128, PITCH, 128), F32),
        pltpu.VMEM((slots // 2, 3, 12, 128, 256), BF16),
        pltpu.VMEM((slots // 2, 3, 10, 128, 256), BF16),
    ]


def teacher_outer(brick, z, count, feats, gauss, w1, w2):
    slots = feats.shape[0]
    return pl.pallas_call(
        outer_kernel,
        name="teacher_outer",
        grid_spec=pltpu.PrefetchScalarGridSpec(
            num_scalar_prefetch=3,
            in_specs=[HBM] * 4,
            out_specs=[VMEM] * 6,
            scratch_shapes=[pltpu.VMEM(w1.shape, BF16), pltpu.VMEM(w2.shape, BF16)]
            + teacher_scratch(slots)
            + [pltpu.VMEM((2, 8, 64, 256), F32), pltpu.SemaphoreType.DMA((slots + 3,))],
        ),
        out_shape=[
            SUMS,
            SUMS,
            jax.ShapeDtypeStruct((256, 1536), BF16),
            jax.ShapeDtypeStruct((128, 1536), BF16),
            jax.ShapeDtypeStruct(feats.shape, BF16),
            jax.ShapeDtypeStruct(gauss.shape, F32),
        ],
        compiler_params=params(28),
        cost_estimate=cost(5_000_000_000, 4_000_000),
    )(*map(in_hbm, (brick, z, count, feats, gauss, w1, w2)))


def teacher_own(brick, z, count, feats, gauss, big1, big2):
    return pl.pallas_call(
        own_kernel,
        name="teacher_own",
        grid_spec=pltpu.PrefetchScalarGridSpec(
            num_scalar_prefetch=3,
            in_specs=[VMEM] * 4,
            out_specs=VMEM,
            scratch_shapes=teacher_scratch(feats.shape[0]),
        ),
        out_shape=SUMS,
        compiler_params=params(28),
        cost_estimate=cost(4_000_000_000, 3_000_000),
    )(*map(in_hbm, (brick, z, count)), feats, gauss, big1, big2)


def relay_kernel(feats_hbm, behind, main_ref, pair_ref, cross_ref, feats_ref, flat, sems):
    odd = parity()
    chunks = 4
    rows = 1024 // chunks
    loads = []
    for i in range(chunks):
        part = pl.ds(i * rows, rows)
        loads.append(pltpu.make_async_copy(feats_hbm.at[part], feats_ref.at[part], sems.at[i]))
        loads[i].start()
    for i in range(chunks):
        loads[i].wait()
        part = pl.ds(i * rows, rows)
        for h in range(2):
            flat[h, part] = feats_ref[part, pl.ds(h * 128, 128)].astype(F32)
            for y in range(8):
                main_ref[y, pl.ds(i * rows // 8, rows // 8), pl.ds(h * 128, 128)] = flat[
                    h, pl.ds(i * rows + y, rows // 8, stride=8), :
                ].astype(BF16)
    pair_ref[...] = main_ref[pl.ds(6 * (1 - odd), 2)]
    cross_ref[...] = main_ref[pl.ds(6 * odd, 2)]


def relay(feats, behind):
    edge = jax.ShapeDtypeStruct((2, 128, 256), BF16)
    return pl.pallas_call(
        relay_kernel,
        name="relay",
        in_specs=[HBM, VMEM],
        out_specs=[VMEM] * 3,
        out_shape=[jax.ShapeDtypeStruct((8, 128, 256), BF16), edge, edge],
        scratch_shapes=[
            pltpu.VMEM((1024, 256), BF16),
            pltpu.VMEM((2, 1024, 128), F32),
            pltpu.SemaphoreType.DMA((4,)),
        ],
        compiler_params=params(8),
        cost_estimate=cost(0, 1_500_000),
    )(in_hbm(feats), behind)


def put_edges(store, pair_ref, cross_ref, low, high):
    odd = parity()
    for k in range(2):
        pair, cross = pair_ref[k].astype(F32), cross_ref[k].astype(F32)
        store(low + k, jnp.where(odd == 1, pair, cross))
        store(high + k, jnp.where(odd == 1, cross, pair))


def inside(y):
    position = lax.axis_index("gy")
    last = lax.axis_size("gy") - 1
    if y < 0:
        return jnp.where(position > 0, 1.0, 0.0)
    if y >= 8:
        return jnp.where(position < last, 1.0, 0.0)
    return None


def class_softmax(v):
    parts = []
    for x in range(4):
        block = v[x * 16 : (x + 1) * 16]
        peak = jnp.max(block, axis=0, keepdims=True)
        grown = jnp.exp(block - peak)
        parts.append(grown * (1.0 / jnp.sum(grown, axis=0, keepdims=True)))
    return jnp.concatenate(parts, axis=0)


def activate(pre):
    sig = sigmoid(pre)
    return pre * sig, sig * (1.0 + pre * (1.0 - sig))


def forward_kernel(main_ref, w1_ref, w2_ref, prob_ref, slope_ref, hbuf, big1, big2, xbuf):
    fill_big(big1, band(w1_ref, False), 2)
    fill_big(big2, band(w2_ref, True), 2)
    for y in range(4):
        put_row(xbuf, y, main_ref[y].astype(F32))
    for y in range(0, 6, 2):
        pre = jnp.dot(big1[...], window(xbuf, y, 4), preferred_element_type=F32)
        if y < 4:
            for k in range(4, 6):
                put_row(xbuf, y + k, main_ref[y + k].astype(F32))
        hid, slope = activate(pre)
        for k in range(2):
            rows = slice(k * 128, (k + 1) * 128)
            slope_ref[y + k] = slope[rows]
            put_row(hbuf, y + k, hid[rows])
    for y in range(0, 4, 2):
        logits = jnp.dot(big2[...], window(hbuf, y, 4), preferred_element_type=F32)
        for k in range(2):
            prob_ref[y + k] = class_softmax(logits[k * 64 : (k + 1) * 64])


def forward(main, w1, w2):
    return pl.pallas_call(
        forward_kernel,
        name="forward",
        in_specs=[VMEM] * 3,
        out_specs=[VMEM] * 5,
        out_shape=[
            jax.ShapeDtypeStruct((4, 64, 256), F32),
            jax.ShapeDtypeStruct((6, 128, 256), F32),
            jax.ShapeDtypeStruct((3, 6, 128, 256), BF16),
            jax.ShapeDtypeStruct((256, 1536), BF16),
            jax.ShapeDtypeStruct((128, 1536), BF16),
        ],
        scratch_shapes=[pltpu.VMEM((3, 8, 128, 256), BF16)],
        compiler_params=params(16),
        cost_estimate=cost(4_000_000_000, 3_000_000),
    )(main, w1, w2)


def edge_kernel(
    main_ref,
    pair_in,
    cross_in,
    hin_ref,
    big1,
    big2,
    own_ref,
    from_pair_ref,
    from_cross_ref,
    pair_ref,
    cross_ref,
    grad_ref,
    slope_ref,
    xbuf,
    hbuf,
):
    put_edges(lambda y, v: put_row(xbuf, y, v), pair_in, cross_in, 0, 6)
    for y, row in ((2, 0), (3, 1), (4, 6), (5, 7)):
        put_row(xbuf, y, main_ref[row].astype(F32))
    for d in range(3):
        hbuf[d, pl.ds(2, 2)] = hin_ref[d, pl.ds(0, 2)]
        hbuf[d, pl.ds(4, 2)] = hin_ref[d, pl.ds(4, 2)]
    for g, h, row in ((0, 0, -1), (4, 6, 7)):
        pre = jnp.dot(big1[...], window(xbuf, g, 4), preferred_element_type=F32)
        hid, slope = activate(pre)
        for k in range(2):
            rows = slice(k * 128, (k + 1) * 128)
            slope_ref[g // 2 + k] = slope[rows]
            keep = inside(row + k)
            put_row(hbuf, h + k, hid[rows] if keep is None else hid[rows] * keep)
    for g, row in ((0, 0), (4, 6)):
        logits = jnp.dot(big2[...], window(hbuf, g, 4), preferred_element_type=F32)
        for k in range(2):
            y = row + k
            value = own_ref[y] + from_pair_ref[y] + from_cross_ref[y]
            prob = class_softmax(logits[k * 64 : (k + 1) * 64])
            grad_ref[g // 2 + k] = (prob - class_softmax(value)).astype(BF16)
    odd = parity()
    pair_ref[...] = grad_ref[pl.ds(2 * (1 - odd), 2)]
    cross_ref[...] = grad_ref[pl.ds(2 * odd, 2)]


def edge_grads(main, pair, cross, hidden, big1, big2, own, from_pair, from_cross):
    edge = jax.ShapeDtypeStruct((2, 64, 256), BF16)
    return pl.pallas_call(
        edge_kernel,
        name="edge_grads",
        in_specs=[VMEM] * 9,
        out_specs=[VMEM] * 4,
        out_shape=[
            edge,
            edge,
            jax.ShapeDtypeStruct((4, 64, 256), BF16),
            jax.ShapeDtypeStruct((4, 128, 256), F32),
        ],
        scratch_shapes=[
            pltpu.VMEM((3, 8, 128, 256), BF16),
            pltpu.VMEM((3, 8, 128, 256), BF16),
        ],
        compiler_params=params(12),
        cost_estimate=cost(2_000_000_000, 3_000_000),
    )(main, pair, cross, hidden, big1, big2, own, from_pair, from_cross)


def put_out(turns, y, grad):
    for k in range(2):
        for x in range(4):
            for h, turn in enumerate(turns):
                at = k * 128 + x * 32
                turn[pl.ds(x * 8 + y + k, 32, stride=32), :] = grad[
                    at : at + 32, h * 128 : (h + 1) * 128
                ]


def inner_kernel(
    own_ref,
    from_pair_ref,
    from_cross_ref,
    prob_ref,
    grad_ref,
    slope_ref,
    w1_ref,
    w2_ref,
    sum_hbm,
    turn0,
    turn1,
    pbuf,
    big1,
    big2,
    gbuf,
    sum0,
    sum1,
    sum_ref,
    sem,
):
    for y in range(8):
        value = own_ref[y] + from_pair_ref[y] + from_cross_ref[y]
        for x in range(4):
            for h, turn in enumerate((sum0, sum1)):
                turn[pl.ds(x * 8 + y, 16, stride=32), :] = value[
                    x * 16 : (x + 1) * 16, h * 128 : (h + 1) * 128
                ]
        if 2 <= y < 6:
            grad = (prob_ref[y - 2] - class_softmax(value)).astype(BF16)
        else:
            grad = grad_ref[y if y < 2 else y - 4]
        put_row(gbuf, y, grad.astype(F32))
    sum_ref[:, pl.ds(0, 128)] = sum0[...]
    sum_ref[:, pl.ds(128, 128)] = sum1[...]
    copy = pltpu.make_async_copy(sum_ref, sum_hbm, sem)
    copy.start()
    flip2 = band(w2_ref, True)
    fill_big(big2, [flip2[8 - t].T for t in range(9)], 2)
    flip1 = band(w1_ref, True)
    fill_big(big1, [flip1[8 - t].T for t in range(9)], 2)
    for y in range(0, 6, 2):
        grad = jnp.dot(big2[...], window(gbuf, y, 4), preferred_element_type=F32)
        for k in range(2):
            put_row(pbuf, y + k, grad[k * 128 : (k + 1) * 128] * slope_ref[y + k])
    for y in range(0, 4, 2):
        grad = jnp.dot(big1[...], window(pbuf, y, 4), preferred_element_type=F32)
        put_out((turn0, turn1), y + 2, grad)
    copy.wait()


def inner(own, from_pair, from_cross, prob, grad, slope, w1, w2):
    turned = jax.ShapeDtypeStruct((1024, 128), F32)
    return pl.pallas_call(
        inner_kernel,
        name="inner",
        in_specs=[VMEM] * 8,
        out_specs=[HBM] + [VMEM] * 5,
        out_shape=[
            jax.ShapeDtypeStruct((512, 256), F32),
            turned,
            turned,
            jax.ShapeDtypeStruct((3, 6, 128, 256), BF16),
            jax.ShapeDtypeStruct((256, 1536), BF16),
            jax.ShapeDtypeStruct((256, 768), BF16),
        ],
        scratch_shapes=[
            pltpu.VMEM((3, 8, 64, 256), BF16),
            pltpu.VMEM((512, 128), F32),
            pltpu.VMEM((512, 128), F32),
            pltpu.VMEM((512, 256), F32),
            pltpu.SemaphoreType.DMA,
        ],
        compiler_params=params(16),
        cost_estimate=cost(4_000_000_000, 3_000_000),
    )(own, from_pair, from_cross, prob, grad, slope, w1, w2)


def outer_rows_kernel(
    main_ref,
    pair_ref,
    cross_ref,
    slope_ref,
    done0,
    done1,
    pin_ref,
    big1,
    big2,
    out_hbm,
    gbuf,
    pbuf,
    turn0,
    turn1,
    out_ref,
    sems,
):
    store = lambda y, v: put_row(gbuf, y, v)
    put_edges(store, pair_ref, cross_ref, 0, 6)
    for y in range(4):
        store(y + 2, main_ref[y].astype(F32))
    for d in range(3):
        pbuf[d, pl.ds(2, 2)] = pin_ref[d, pl.ds(0, 2)]
        pbuf[d, pl.ds(4, 2)] = pin_ref[d, pl.ds(4, 2)]
    for g, p, row in ((0, 0, -1), (4, 6, 7)):
        grad = jnp.dot(big2[...], window(gbuf, g, 4), preferred_element_type=F32)
        for k in range(2):
            v = grad[k * 128 : (k + 1) * 128] * slope_ref[g // 2 + k]
            keep = inside(row + k)
            put_row(pbuf, p + k, v if keep is None else v * keep)
    for p, row in ((0, 0), (4, 6)):
        grad = jnp.dot(big1[...], window(pbuf, p, 4), preferred_element_type=F32)
        put_out((turn0, turn1), row, grad)
    chunks = 4
    rows = 1024 // chunks
    y = lax.broadcasted_iota(jnp.int32, (rows, 128), 0) % 8
    early = (y >= 2) & (y < 6)
    copies = []
    for i in range(chunks):
        part = pl.ds(i * rows, rows)
        out_ref[part, pl.ds(0, 128)] = jnp.where(early, done0[part], turn0[part])
        out_ref[part, pl.ds(128, 128)] = jnp.where(early, done1[part], turn1[part])
        copies.append(pltpu.make_async_copy(out_ref.at[part], out_hbm.at[part], sems.at[i]))
        copies[i].start()
    for copy in copies:
        copy.wait()


def outer_rows(main, pair, cross, slope, done0, done1, pin, big1, big2):
    return pl.pallas_call(
        outer_rows_kernel,
        name="outer_rows",
        in_specs=[VMEM] * 9,
        out_specs=HBM,
        out_shape=jax.ShapeDtypeStruct((1024, 256), F32),
        scratch_shapes=[
            pltpu.VMEM((3, 8, 64, 256), BF16),
            pltpu.VMEM((3, 8, 128, 256), BF16),
            pltpu.VMEM((1024, 128), F32),
            pltpu.VMEM((1024, 128), F32),
            pltpu.VMEM((1024, 256), F32),
            pltpu.SemaphoreType.DMA((4,)),
        ],
        compiler_params=params(16),
        cost_estimate=cost(2_000_000_000, 3_000_000),
    )(main, pair, cross, slope, done0, done1, pin, big1, big2)


def swap_pair(value):
    count = lax.axis_size("gy")
    return lax.ppermute(value, "gy", [(i, i ^ 1) for i in range(count)])


def swap_cross(value):
    count = lax.axis_size("gy")
    pairs = [(i, i + 1) for i in range(1, count - 1, 2)]
    return lax.ppermute(value, "gy", pairs + [(j, i) for i, j in pairs])


def taps_first(w):
    outs, ins = w.shape[:2]
    return jnp.transpose(w, (2, 3, 4, 0, 1)).reshape(3, 9, outs, ins)


def body(
    window_feats,
    window_brick,
    window_z,
    window_count,
    gaussian,
    brick_feats,
    teacher_w1,
    teacher_w2,
    student_w1,
    student_w2,
):
    tw1, tw2, sw1, sw2 = map(taps_first, (teacher_w1, teacher_w2, student_w1, student_w2))
    feats = window_feats.reshape(window_feats.shape[0], 2048, 128)
    tables = (window_brick, window_z, window_count)
    sum_pair, sum_cross, *kept = teacher_outer(*tables, feats, gaussian, tw1, tw2)
    big1, big2, held_feats, held_gauss = kept
    got_pair = swap_pair(sum_pair)
    got_cross = swap_cross(sum_cross)
    main, to_pair, to_cross = relay(brick_feats.reshape(1024, 256), held_gauss)
    edge_pair = swap_pair(to_pair)
    edge_cross = swap_cross(to_cross)
    own = teacher_own(*tables, held_feats, held_gauss, big1, big2)
    prob, slope, hidden, *bigs = forward(main, sw1, sw2)
    sums = (own, got_pair, got_cross)
    grad_pair, grad_cross, grad, slope_ends = edge_grads(
        main, edge_pair, edge_cross, hidden, *bigs, *sums
    )
    near_pair = swap_pair(grad_pair)
    near_cross = swap_cross(grad_cross)
    teacher_sum, *early = inner(*sums, prob, grad, slope, sw1, sw2)
    feature_grad = outer_rows(grad, near_pair, near_cross, slope_ends, *early)
    return (teacher_sum.reshape(16, 4, 8, 256), feature_grad.reshape(32, 4, 8, 256))


def solution(mesh):
    placed = (
        P(("grp", "gy"), None, None, None, None),
        P("grp"),
        P("grp"),
        P("grp"),
        P(),
        P(None, None, ("grp", "gy"), None),
        P(),
        P(),
        P(),
        P(),
    )
    return jax.shard_map(
        body,
        mesh=mesh,
        in_specs=placed,
        out_specs=(P(None, None, ("grp", "gy"), None), P(None, None, ("grp", "gy"), None)),
        check_vma=False,
    )
```

```python
import functools

import jax
import jax.numpy as jnp
from jax import lax
from jax.experimental import pallas as pl
from jax.experimental.pallas import tpu as pltpu
from jax.sharding import PartitionSpec as P

F32 = jnp.float32
PITCH = 24
BF16 = jnp.bfloat16
VMEM = pl.BlockSpec(memory_space=pltpu.VMEM)
HBM = pl.BlockSpec(memory_space=pltpu.HBM)


def in_hbm(value):
    return pltpu.with_memory_space_constraint(value, pltpu.HBM)


def params(mib):
    return pltpu.CompilerParams(vmem_limit_bytes=mib * 1024 * 1024)


def cost(flops, moved):
    return pl.CostEstimate(flops=flops, bytes_accessed=moved, transcendentals=0)


def spread(ins, a, by_x):
    c = lax.broadcasted_iota(jnp.int32, (ins, 16 * ins), 0)
    lane = lax.broadcasted_iota(jnp.int32, (ins, 16 * ins), 1)
    x = lane // (4 * ins)
    rest = lane % (4 * ins)
    if by_x:
        xi, ci = rest // ins, rest % ins
    else:
        xi, ci = rest % 4, rest // 4
    return jnp.where((ci == c) & (xi == x + a - 1), 1.0, 0.0).astype(BF16)


def band(w_ref, by_x):
    _, taps, outs, ins = w_ref.shape
    wide = None
    for a in range(3):
        part = jnp.dot(
            w_ref[a].reshape(taps * outs, ins),
            spread(ins, a, by_x),
            preferred_element_type=F32,
        )
        wide = part if wide is None else wide + part
    width = 4 * ins
    result = []
    for t in range(taps):
        rows = wide[t * outs : (t + 1) * outs]
        result.append(
            jnp.concatenate(
                [rows[:, x * width : (x + 1) * width] for x in range(4)], axis=0
            )
        )
    return result


def fill_big(big_ref, blocks, out_rows):
    rows, width = blocks[0].shape
    in_rows = out_rows + 2
    zero = jnp.zeros((rows, width), BF16)
    for yo in range(out_rows):
        for d in range(3):
            for yi in range(in_rows):
                b = yi - yo
                piece = blocks[b * 3 + d].astype(BF16) if 0 <= b < 3 else zero
                col = (d * in_rows + yi) * width
                big_ref[pl.ds(yo * rows, rows), pl.ds(col, width)] = piece


def shifted(v, step):
    lanes = v.shape[-1]
    rolled = pltpu.roll(v, (-step) % lanes, v.ndim - 1)
    lane = lax.broadcasted_iota(jnp.int32, v.shape, v.ndim - 1)
    edge = lane == (lanes - 1 if step > 0 else 0)
    return jnp.where(edge, 0.0, rolled)


def put_row(buf_ref, y, v, lane=0):
    lanes = pl.ds(lane, v.shape[-1])
    buf_ref[1, y, :, lanes] = v.astype(BF16)
    buf_ref[0, y, :, lanes] = shifted(v, -1).astype(BF16)
    buf_ref[2, y, :, lanes] = shifted(v, 1).astype(BF16)


def window(buf_ref, y, count):
    rows = buf_ref.shape[2]
    return jnp.concatenate(
        [buf_ref[d, pl.ds(y, count)].reshape(count * rows, -1) for d in range(3)], axis=0
    )


def sigmoid(v):
    return 0.5 + 0.5 * jnp.tanh(0.5 * v)


def parity():
    return lax.rem(lax.axis_index("gy"), 2)


def teacher_half(
    own, tables, ready, feats_ref, gauss_ref, big1, big2, store, flat, xbuf, hbuf
):
    brick_s, z_s, count_s = tables
    position = lax.axis_index("gy")
    slots = feats_ref.shape[0]
    lanes = 128
    count = count_s[position]
    lane = lax.broadcasted_iota(jnp.int32, (64, lanes), 1)
    z0, mine, base = [], [], []
    for s in range(slots):
        slot = position * slots + s
        z0.append(z_s[slot])
        mine.append(brick_s[slot] == position)
        base.append(jnp.where(mine[s], 0, 8) if own else jnp.where(mine[s], 8, 0))
    low_end = [jnp.where(base[s] == 0, 0.0, 1.0) for s in range(slots)]
    high_end = [jnp.where(base[s] == 8, 0.0, 1.0) for s in range(slots)]
    emitted = set()
    value = {}

    def unpack(s):
        if ("u", s) not in emitted:
            emitted.add(("u", s))
            ready(s)
            flat[s, :, pl.ds(0, 16)] = feats_ref[s].astype(F32).reshape(128, 16, 128)

    def x_row(duo, q):
        if ("x", duo, q) in emitted:
            return
        emitted.add(("x", duo, q))
        for k in range(2):
            s = 2 * duo + k
            unpack(s)
            row = jnp.clip(base[s] - 2 + q, 0, 15)
            v = flat.at[s].reshape(128 * PITCH, 128)[pl.ds(row, 128, stride=PITCH), :]
            if q < 2:
                v = v * low_end[s]
            if q > 9:
                v = v * high_end[s]
            put_row(xbuf.at[duo], q, v, k * lanes)

    def before(op):
        kind, duo, q = op
        if kind == "hidden":
            for r in range(q, q + 4):
                x_row(duo, r)

    def product(op):
        kind, duo, q = op
        if kind == "hidden":
            big, data = big1, window(xbuf.at[duo], q, 4)
        else:
            big, data = big2, window(hbuf.at[duo], q, 4)
        value[op] = jnp.dot(big[...], data, preferred_element_type=F32)

    def after(op):
        kind, duo, q = op
        out = value.pop(op)
        if kind == "hidden":
            hid = out * sigmoid(out)
            for r in range(2):
                for k in range(2):
                    v = hid[r * 128 : (r + 1) * 128, k * lanes : (k + 1) * lanes]
                    if q + r == 0:
                        v = v * low_end[2 * duo + k]
                    if q + r == 9:
                        v = v * high_end[2 * duo + k]
                    put_row(hbuf.at[duo], q + r, v, k * lanes)
            return
        for k in range(2):
            s = 2 * duo + k
            live = jnp.where(s < count, 1.0, 0.0)
            keep = lane >= z0[s]
            for r in range(2):
                part = out[r * 64 : (r + 1) * 64, k * lanes : (k + 1) * lanes]
                weight = jnp.concatenate(
                    [
                        jnp.broadcast_to(
                            gauss_ref[x, pl.ds(base[s] + q + r, 1), :] * live, (16, lanes)
                        )
                        for x in range(4)
                    ],
                    axis=0,
                )
                turned = pltpu.roll(part * weight, lax.rem(z0[s], 128), 1)
                store(mine[s], q + r, jnp.where(keep, turned, 0.0), jnp.where(keep, 0.0, turned))

    order = []
    late = []
    for duo in range(slots // 2):
        for q in range(0, 10, 2):
            order.append(("hidden", duo, q))
            if late:
                order.append(late.pop(0))
        late = [("logits", duo, q) for q in range(0, 8, 2)]
    order += late
    before(order[0])
    before(order[1])
    for i, op in enumerate(order):
        product(op)
        if i > 0:
            after(order[i - 1])
        if i + 2 < len(order):
            before(order[i + 2])
    after(order[-1])


def outer_kernel(
    brick_s,
    z_s,
    count_s,
    feats_hbm,
    gauss_hbm,
    w1_hbm,
    w2_hbm,
    cross_ref,
    total,
    big1,
    big2,
    feats_ref,
    gauss_ref,
    w1_ref,
    w2_ref,
    flat,
    xbuf,
    hbuf,
    sems,
):
    slots = feats_ref.shape[0]
    copies = [
        pltpu.make_async_copy(w1_hbm, w1_ref, sems.at[slots]),
        pltpu.make_async_copy(w2_hbm, w2_ref, sems.at[slots + 1]),
        pltpu.make_async_copy(gauss_hbm, gauss_ref, sems.at[slots + 2]),
    ]
    for copy in copies:
        copy.start()
    loads = [
        pltpu.make_async_copy(feats_hbm.at[s], feats_ref.at[s], sems.at[s]) for s in range(slots)
    ]
    for load in loads:
        load.start()
    total[...] = jnp.zeros_like(total)
    for copy in copies:
        copy.wait()
    fill_big(big1, band(w1_ref, False), 2)
    fill_big(big2, band(w2_ref, True), 2)

    def store(mine, row, low, high):
        side = jnp.where(mine, 1, 0)
        total[side, row, :, pl.ds(0, 128)] += low
        total[side, row, :, pl.ds(128, 128)] += high

    teacher_half(
        False,
        (brick_s, z_s, count_s),
        lambda s: loads[s].wait(),
        feats_ref,
        gauss_ref,
        big1,
        big2,
        store,
        flat,
        xbuf,
        hbuf,
    )
    cross_ref[...] = total[parity()]


def own_kernel(
    brick_s,
    z_s,
    count_s,
    feats_ref,
    gauss_ref,
    big1,
    big2,
    total,
    main_ref,
    own_ref,
    pair_ref,
    edge_ref,
    flat,
    xbuf,
    hbuf,
):
    own_ref[...] = jnp.zeros_like(own_ref)
    odd = parity()
    pair_ref[...] = total[1 - odd]
    edge_ref[...] = main_ref[pl.ds(6 * (1 - odd), 2)]

    def store(mine, row, low, high):
        own_ref[row, :, pl.ds(0, 128)] += low
        own_ref[row, :, pl.ds(128, 128)] += high

    teacher_half(
        True,
        (brick_s, z_s, count_s),
        lambda s: None,
        feats_ref,
        gauss_ref,
        big1,
        big2,
        store,
        flat,
        xbuf,
        hbuf,
    )


SUMS = jax.ShapeDtypeStruct((8, 64, 256), F32)
EDGE = jax.ShapeDtypeStruct((2, 128, 256), BF16)


def teacher_scratch(slots):
    return [
        pltpu.VMEM((slots, 128, PITCH, 128), F32),
        pltpu.VMEM((slots // 2, 3, 12, 128, 256), BF16),
        pltpu.VMEM((slots // 2, 3, 10, 128, 256), BF16),
    ]


def teacher_outer(brick, z, count, feats, gauss, w1, w2):
    slots = feats.shape[0]
    return pl.pallas_call(
        outer_kernel,
        name="teacher_outer",
        grid_spec=pltpu.PrefetchScalarGridSpec(
            num_scalar_prefetch=3,
            in_specs=[HBM] * 4,
            out_specs=[VMEM] * 6,
            scratch_shapes=[pltpu.VMEM(w1.shape, BF16), pltpu.VMEM(w2.shape, BF16)]
            + teacher_scratch(slots)
            + [pltpu.SemaphoreType.DMA((slots + 3,))],
        ),
        out_shape=[
            SUMS,
            jax.ShapeDtypeStruct((2, 8, 64, 256), F32),
            jax.ShapeDtypeStruct((256, 1536), BF16),
            jax.ShapeDtypeStruct((128, 1536), BF16),
            jax.ShapeDtypeStruct(feats.shape, BF16),
            jax.ShapeDtypeStruct(gauss.shape, F32),
        ],
        compiler_params=params(28),
        cost_estimate=cost(5_000_000_000, 4_000_000),
    )(*map(in_hbm, (brick, z, count, feats, gauss, w1, w2)))


def teacher_own(brick, z, count, feats, gauss, big1, big2, total, main):
    return pl.pallas_call(
        own_kernel,
        name="teacher_own",
        grid_spec=pltpu.PrefetchScalarGridSpec(
            num_scalar_prefetch=3,
            in_specs=[VMEM] * 6,
            out_specs=[VMEM] * 3,
            scratch_shapes=teacher_scratch(feats.shape[0]),
        ),
        out_shape=[SUMS, SUMS, EDGE],
        compiler_params=params(28),
        cost_estimate=cost(4_000_000_000, 3_000_000),
    )(*map(in_hbm, (brick, z, count)), feats, gauss, big1, big2, total, main)


def relay_kernel(feats_hbm, behind, main_ref, cross_ref, feats_ref, flat, sems):
    chunks = 4
    rows = 1024 // chunks
    loads = []
    for i in range(chunks):
        part = pl.ds(i * rows, rows)
        loads.append(pltpu.make_async_copy(feats_hbm.at[part], feats_ref.at[part], sems.at[i]))
        loads[i].start()
    for i in range(chunks):
        loads[i].wait()
        part = pl.ds(i * rows, rows)
        for h in range(2):
            flat[h, part] = feats_ref[part, pl.ds(h * 128, 128)].astype(F32)
            for y in range(8):
                main_ref[y, pl.ds(i * rows // 8, rows // 8), pl.ds(h * 128, 128)] = flat[
                    h, pl.ds(i * rows + y, rows // 8, stride=8), :
                ].astype(BF16)
    cross_ref[...] = main_ref[pl.ds(6 * parity(), 2)]


def relay(feats, behind):
    return pl.pallas_call(
        relay_kernel,
        name="relay",
        in_specs=[HBM, VMEM],
        out_specs=[VMEM] * 2,
        out_shape=[jax.ShapeDtypeStruct((8, 128, 256), BF16), EDGE],
        scratch_shapes=[
            pltpu.VMEM((1024, 256), BF16),
            pltpu.VMEM((2, 1024, 128), F32),
            pltpu.SemaphoreType.DMA((4,)),
        ],
        compiler_params=params(8),
        cost_estimate=cost(0, 1_500_000),
    )(in_hbm(feats), behind)


def put_edges(store, pair_ref, cross_ref, low, high):
    odd = parity()
    for k in range(2):
        pair, cross = pair_ref[k].astype(F32), cross_ref[k].astype(F32)
        store(low + k, jnp.where(odd == 1, pair, cross))
        store(high + k, jnp.where(odd == 1, cross, pair))


def inside(y):
    position = lax.axis_index("gy")
    last = lax.axis_size("gy") - 1
    if y < 0:
        return jnp.where(position > 0, 1.0, 0.0)
    if y >= 8:
        return jnp.where(position < last, 1.0, 0.0)
    return None


def class_softmax(v):
    parts = []
    for x in range(4):
        block = v[x * 16 : (x + 1) * 16]
        peak = jnp.max(block, axis=0, keepdims=True)
        grown = jnp.exp(block - peak)
        parts.append(grown * (1.0 / jnp.sum(grown, axis=0, keepdims=True)))
    return jnp.concatenate(parts, axis=0)


def activate(pre):
    sig = sigmoid(pre)
    return pre * sig, sig * (1.0 + pre * (1.0 - sig))


def forward_kernel(
    main_ref, w1_ref, w2_ref, prob_ref, slope_ref, hbuf, big1, big2, back1, back2, xbuf
):
    fill_big(big1, band(w1_ref, False), 2)
    fill_big(big2, band(w2_ref, True), 2)
    for y in range(4):
        put_row(xbuf, y, main_ref[y].astype(F32))
    for y in range(0, 6, 2):
        pre = jnp.dot(big1[...], window(xbuf, y, 4), preferred_element_type=F32)
        if y < 4:
            for k in range(4, 6):
                put_row(xbuf, y + k, main_ref[y + k].astype(F32))
        hid, slope = activate(pre)
        for k in range(2):
            rows = slice(k * 128, (k + 1) * 128)
            slope_ref[y + k] = slope[rows]
            put_row(hbuf, y + k, hid[rows])
    for y in range(0, 4, 2):
        logits = jnp.dot(big2[...], window(hbuf, y, 4), preferred_element_type=F32)
        for k in range(2):
            prob_ref[y + k] = class_softmax(logits[k * 64 : (k + 1) * 64])
    flip2 = band(w2_ref, True)
    fill_big(back2, [flip2[8 - t].T for t in range(9)], 2)
    flip1 = band(w1_ref, True)
    fill_big(back1, [flip1[8 - t].T for t in range(9)], 2)


def forward(main, w1, w2):
    return pl.pallas_call(
        forward_kernel,
        name="forward",
        in_specs=[VMEM] * 3,
        out_specs=[VMEM] * 7,
        out_shape=[
            jax.ShapeDtypeStruct((4, 64, 256), F32),
            jax.ShapeDtypeStruct((6, 128, 256), F32),
            jax.ShapeDtypeStruct((3, 6, 128, 256), BF16),
            jax.ShapeDtypeStruct((256, 1536), BF16),
            jax.ShapeDtypeStruct((128, 1536), BF16),
            jax.ShapeDtypeStruct((256, 1536), BF16),
            jax.ShapeDtypeStruct((256, 768), BF16),
        ],
        scratch_shapes=[pltpu.VMEM((3, 8, 128, 256), BF16)],
        compiler_params=params(16),
        cost_estimate=cost(4_000_000_000, 3_000_000),
    )(main, w1, w2)


def edge_kernel(
    main_ref,
    cross_in,
    pair_in,
    hin_ref,
    big1,
    big2,
    own_ref,
    from_pair_ref,
    from_cross_ref,
    pair_ref,
    cross_ref,
    grad_ref,
    slope_ref,
    xbuf,
    hbuf,
):
    put_edges(lambda y, v: put_row(xbuf, y, v), pair_in, cross_in, 0, 6)
    for y, row in ((2, 0), (3, 1), (4, 6), (5, 7)):
        put_row(xbuf, y, main_ref[row].astype(F32))
    for d in range(3):
        hbuf[d, pl.ds(2, 2)] = hin_ref[d, pl.ds(0, 2)]
        hbuf[d, pl.ds(4, 2)] = hin_ref[d, pl.ds(4, 2)]
    for g, h, row in ((0, 0, -1), (4, 6, 7)):
        pre = jnp.dot(big1[...], window(xbuf, g, 4), preferred_element_type=F32)
        hid, slope = activate(pre)
        for k in range(2):
            rows = slice(k * 128, (k + 1) * 128)
            slope_ref[g // 2 + k] = slope[rows]
            keep = inside(row + k)
            put_row(hbuf, h + k, hid[rows] if keep is None else hid[rows] * keep)
    for g, row in ((0, 0), (4, 6)):
        logits = jnp.dot(big2[...], window(hbuf, g, 4), preferred_element_type=F32)
        for k in range(2):
            y = row + k
            value = own_ref[y] + from_pair_ref[y] + from_cross_ref[y]
            prob = class_softmax(logits[k * 64 : (k + 1) * 64])
            grad_ref[g // 2 + k] = (prob - class_softmax(value)).astype(BF16)
    odd = parity()
    pair_ref[...] = grad_ref[pl.ds(2 * (1 - odd), 2)]
    cross_ref[...] = grad_ref[pl.ds(2 * odd, 2)]


def edge_grads(main, cross, pair, hidden, big1, big2, own, from_pair, from_cross):
    edge = jax.ShapeDtypeStruct((2, 64, 256), BF16)
    return pl.pallas_call(
        edge_kernel,
        name="edge_grads",
        in_specs=[VMEM] * 9,
        out_specs=[VMEM] * 4,
        out_shape=[
            edge,
            edge,
            jax.ShapeDtypeStruct((4, 64, 256), BF16),
            jax.ShapeDtypeStruct((4, 128, 256), F32),
        ],
        scratch_shapes=[
            pltpu.VMEM((3, 8, 128, 256), BF16),
            pltpu.VMEM((3, 8, 128, 256), BF16),
        ],
        compiler_params=params(12),
        cost_estimate=cost(2_000_000_000, 3_000_000),
    )(main, cross, pair, hidden, big1, big2, own, from_pair, from_cross)


def put_out(turns, y, grad):
    for k in range(2):
        for x in range(4):
            for h, turn in enumerate(turns):
                at = k * 128 + x * 32
                turn[pl.ds(x * 8 + y + k, 32, stride=32), :] = grad[
                    at : at + 32, h * 128 : (h + 1) * 128
                ]


def inner_kernel(
    own_ref,
    from_pair_ref,
    from_cross_ref,
    prob_ref,
    grad_ref,
    slope_ref,
    big1,
    big2,
    sum_hbm,
    turn0,
    turn1,
    pbuf,
    gbuf,
    sum0,
    sum1,
    sum_ref,
    sem,
):
    for y in range(8):
        value = own_ref[y] + from_pair_ref[y] + from_cross_ref[y]
        for x in range(4):
            for h, turn in enumerate((sum0, sum1)):
                turn[pl.ds(x * 8 + y, 16, stride=32), :] = value[
                    x * 16 : (x + 1) * 16, h * 128 : (h + 1) * 128
                ]
        if 2 <= y < 6:
            grad = (prob_ref[y - 2] - class_softmax(value)).astype(BF16)
        else:
            grad = grad_ref[y if y < 2 else y - 4]
        put_row(gbuf, y, grad.astype(F32))
    sum_ref[:, pl.ds(0, 128)] = sum0[...]
    sum_ref[:, pl.ds(128, 128)] = sum1[...]
    copy = pltpu.make_async_copy(sum_ref, sum_hbm, sem)
    copy.start()
    for y in range(0, 6, 2):
        grad = jnp.dot(big2[...], window(gbuf, y, 4), preferred_element_type=F32)
        for k in range(2):
            put_row(pbuf, y + k, grad[k * 128 : (k + 1) * 128] * slope_ref[y + k])
    for y in range(0, 4, 2):
        grad = jnp.dot(big1[...], window(pbuf, y, 4), preferred_element_type=F32)
        put_out((turn0, turn1), y + 2, grad)
    copy.wait()


def inner(own, from_pair, from_cross, prob, grad, slope, big1, big2):
    turned = jax.ShapeDtypeStruct((1024, 128), F32)
    return pl.pallas_call(
        inner_kernel,
        name="inner",
        in_specs=[VMEM] * 8,
        out_specs=[HBM] + [VMEM] * 3,
        out_shape=[
            jax.ShapeDtypeStruct((512, 256), F32),
            turned,
            turned,
            jax.ShapeDtypeStruct((3, 6, 128, 256), BF16),
        ],
        scratch_shapes=[
            pltpu.VMEM((3, 8, 64, 256), BF16),
            pltpu.VMEM((512, 128), F32),
            pltpu.VMEM((512, 128), F32),
            pltpu.VMEM((512, 256), F32),
            pltpu.SemaphoreType.DMA,
        ],
        compiler_params=params(16),
        cost_estimate=cost(4_000_000_000, 3_000_000),
    )(own, from_pair, from_cross, prob, grad, slope, big1, big2)


def outer_rows_kernel(
    main_ref,
    cross_ref,
    pair_ref,
    slope_ref,
    done0,
    done1,
    pin_ref,
    big1,
    big2,
    out_hbm,
    gbuf,
    pbuf,
    turn0,
    turn1,
    out_ref,
    sems,
):
    store = lambda y, v: put_row(gbuf, y, v)
    put_edges(store, pair_ref, cross_ref, 0, 6)
    for y in range(4):
        store(y + 2, main_ref[y].astype(F32))
    for d in range(3):
        pbuf[d, pl.ds(2, 2)] = pin_ref[d, pl.ds(0, 2)]
        pbuf[d, pl.ds(4, 2)] = pin_ref[d, pl.ds(4, 2)]
    for g, p, row in ((0, 0, -1), (4, 6, 7)):
        grad = jnp.dot(big2[...], window(gbuf, g, 4), preferred_element_type=F32)
        for k in range(2):
            v = grad[k * 128 : (k + 1) * 128] * slope_ref[g // 2 + k]
            keep = inside(row + k)
            put_row(pbuf, p + k, v if keep is None else v * keep)
    y = lax.broadcasted_iota(jnp.int32, (32, 16, 128), 1) % 8
    early = (y >= 2) & (y < 6)
    copies = []
    for i in range(2):
        half = jnp.concatenate([big1[pl.ds(k * 128 + i * 64, 64)] for k in range(2)], axis=0)
        for p, row in ((0, 0), (4, 6)):
            grad = jnp.dot(half, window(pbuf, p, 4), preferred_element_type=F32)
            for k in range(2):
                for x in range(2):
                    for h, turn in enumerate((turn0, turn1)):
                        at = k * 64 + x * 32
                        turn[pl.ds((2 * i + x) * 8 + row + k, 32, stride=32), :] = grad[
                            at : at + 32, h * 128 : (h + 1) * 128
                        ]
        part = pl.ds(i * 16, 16)
        for h, (turn, done) in enumerate(((turn0, done0), (turn1, done1))):
            late = turn.reshape(32, 32, 128)[:, part]
            kept = done.reshape(32, 32, 128)[:, part]
            out_ref[i, :, :, pl.ds(h * 128, 128)] = jnp.where(early, kept, late)
        copies.append(pltpu.make_async_copy(out_ref.at[i], out_hbm.at[:, part], sems.at[i]))
        copies[i].start()
    for copy in copies:
        copy.wait()


def outer_rows(main, cross, pair, slope, done0, done1, pin, big1, big2):
    return pl.pallas_call(
        outer_rows_kernel,
        name="outer_rows",
        in_specs=[VMEM] * 9,
        out_specs=HBM,
        out_shape=jax.ShapeDtypeStruct((32, 32, 256), F32),
        scratch_shapes=[
            pltpu.VMEM((3, 8, 64, 256), BF16),
            pltpu.VMEM((3, 8, 128, 256), BF16),
            pltpu.VMEM((1024, 128), F32),
            pltpu.VMEM((1024, 128), F32),
            pltpu.VMEM((2, 32, 16, 256), F32),
            pltpu.SemaphoreType.DMA((2,)),
        ],
        compiler_params=params(16),
        cost_estimate=cost(2_000_000_000, 3_000_000),
    )(main, cross, pair, slope, done0, done1, pin, big1, big2)


def swap_pair(value):
    count = lax.axis_size("gy")
    return lax.ppermute(value, "gy", [(i, i ^ 1) for i in range(count)])


def swap_cross(value):
    count = lax.axis_size("gy")
    pairs = [(i, i + 1) for i in range(1, count - 1, 2)]
    return lax.ppermute(value, "gy", pairs + [(j, i) for i, j in pairs])


def taps_first(w):
    outs, ins = w.shape[:2]
    return jnp.transpose(w, (2, 3, 4, 0, 1)).reshape(3, 9, outs, ins)


def body(
    window_feats,
    window_brick,
    window_z,
    window_count,
    gaussian,
    brick_feats,
    teacher_w1,
    teacher_w2,
    student_w1,
    student_w2,
):
    tw1, tw2, sw1, sw2 = map(taps_first, (teacher_w1, teacher_w2, student_w1, student_w2))
    feats = window_feats.reshape(window_feats.shape[0], 2048, 128)
    tables = (window_brick, window_z, window_count)
    sum_cross, sides, big1, big2, held_feats, held_gauss = teacher_outer(
        *tables, feats, gaussian, tw1, tw2
    )
    got_cross = swap_cross(sum_cross)
    main, to_cross = relay(brick_feats.reshape(1024, 256), held_gauss)
    edge_cross = swap_cross(to_cross)
    own, sum_pair, to_pair = teacher_own(
        *tables, held_feats, held_gauss, big1, big2, sides, main
    )
    got_pair = swap_pair(sum_pair)
    edge_pair = swap_pair(to_pair)
    prob, slope, hidden, near1, near2, back1, back2 = forward(main, sw1, sw2)
    sums = (own, got_pair, got_cross)
    grad_pair, grad_cross, grad, slope_ends = edge_grads(
        main, edge_cross, edge_pair, hidden, near1, near2, *sums
    )
    near_pair = swap_pair(grad_pair)
    near_cross = swap_cross(grad_cross)
    teacher_sum, *early = inner(*sums, prob, grad, slope, back1, back2)
    feature_grad = outer_rows(grad, near_cross, near_pair, slope_ends, *early, back1, back2)
    return (teacher_sum.reshape(16, 4, 8, 256), feature_grad.reshape(32, 4, 8, 256))


def solution(mesh):
    placed = (
        P(("grp", "gy"), None, None, None, None),
        P("grp"),
        P("grp"),
        P("grp"),
        P(),
        P(None, None, ("grp", "gy"), None),
        P(),
        P(),
        P(),
        P(),
    )
    return jax.shard_map(
        body,
        mesh=mesh,
        in_specs=placed,
        out_specs=(P(None, None, ("grp", "gy"), None), P(None, None, ("grp", "gy"), None)),
        check_vma=False,
    )
```

```python
import functools

import jax
import jax.numpy as jnp
from jax import lax
from jax.experimental import pallas as pl
from jax.experimental.pallas import tpu as pltpu
from jax.sharding import PartitionSpec as P

F32 = jnp.float32
PITCH = 24
BF16 = jnp.bfloat16
VMEM = pl.BlockSpec(memory_space=pltpu.VMEM)
HBM = pl.BlockSpec(memory_space=pltpu.HBM)


def in_hbm(value):
    return pltpu.with_memory_space_constraint(value, pltpu.HBM)


def params(mib):
    return pltpu.CompilerParams(vmem_limit_bytes=mib * 1024 * 1024)


def cost(flops, moved):
    return pl.CostEstimate(flops=flops, bytes_accessed=moved, transcendentals=0)


def spread(ins, a, by_x):
    c = lax.broadcasted_iota(jnp.int32, (ins, 16 * ins), 0)
    lane = lax.broadcasted_iota(jnp.int32, (ins, 16 * ins), 1)
    x = lane // (4 * ins)
    rest = lane % (4 * ins)
    if by_x:
        xi, ci = rest // ins, rest % ins
    else:
        xi, ci = rest % 4, rest // 4
    return jnp.where((ci == c) & (xi == x + a - 1), 1.0, 0.0).astype(BF16)


def band(w_ref, by_x):
    _, taps, outs, ins = w_ref.shape
    wide = None
    for a in range(3):
        part = jnp.dot(
            w_ref[a].reshape(taps * outs, ins),
            spread(ins, a, by_x),
            preferred_element_type=F32,
        )
        wide = part if wide is None else wide + part
    width = 4 * ins
    result = []
    for t in range(taps):
        rows = wide[t * outs : (t + 1) * outs]
        result.append(
            jnp.concatenate(
                [rows[:, x * width : (x + 1) * width] for x in range(4)], axis=0
            )
        )
    return result


def fill_big(big_ref, blocks, out_rows):
    rows, width = blocks[0].shape
    in_rows = out_rows + 2
    zero = jnp.zeros((rows, width), BF16)
    for yo in range(out_rows):
        for d in range(3):
            for yi in range(in_rows):
                b = yi - yo
                piece = blocks[b * 3 + d].astype(BF16) if 0 <= b < 3 else zero
                col = (d * in_rows + yi) * width
                big_ref[pl.ds(yo * rows, rows), pl.ds(col, width)] = piece


def shifted(v, step):
    lanes = v.shape[-1]
    rolled = pltpu.roll(v, (-step) % lanes, v.ndim - 1)
    lane = lax.broadcasted_iota(jnp.int32, v.shape, v.ndim - 1)
    edge = lane == (lanes - 1 if step > 0 else 0)
    return jnp.where(edge, 0.0, rolled)


def put_row(buf_ref, y, v, lane=0):
    lanes = pl.ds(lane, v.shape[-1])
    buf_ref[1, y, :, lanes] = v.astype(BF16)
    buf_ref[0, y, :, lanes] = shifted(v, -1).astype(BF16)
    buf_ref[2, y, :, lanes] = shifted(v, 1).astype(BF16)


def window(buf_ref, y, count):
    rows = buf_ref.shape[2]
    return jnp.concatenate(
        [buf_ref[d, pl.ds(y, count)].reshape(count * rows, -1) for d in range(3)], axis=0
    )


def sigmoid(v):
    return 0.5 + 0.5 * jnp.tanh(0.5 * v)


def parity():
    return lax.rem(lax.axis_index("gy"), 2)


def teacher_half(
    own, tables, ready, feats_ref, gauss_ref, big1, big2, store, flat, xbuf, hbuf
):
    brick_s, z_s, count_s = tables
    position = lax.axis_index("gy")
    slots = feats_ref.shape[0]
    lanes = 128
    count = count_s[position]
    lane = lax.broadcasted_iota(jnp.int32, (64, lanes), 1)
    z0, mine, base = [], [], []
    for s in range(slots):
        slot = position * slots + s
        z0.append(z_s[slot])
        mine.append(brick_s[slot] == position)
        base.append(jnp.where(mine[s], 0, 8) if own else jnp.where(mine[s], 8, 0))
    low_end = [jnp.where(base[s] == 0, 0.0, 1.0) for s in range(slots)]
    high_end = [jnp.where(base[s] == 8, 0.0, 1.0) for s in range(slots)]
    emitted = set()
    value = {}

    def unpack(s):
        if ("u", s) not in emitted:
            emitted.add(("u", s))
            ready(s)
            flat[s, :, pl.ds(0, 16)] = feats_ref[s].astype(F32).reshape(128, 16, 128)

    def x_row(duo, q):
        if ("x", duo, q) in emitted:
            return
        emitted.add(("x", duo, q))
        for k in range(2):
            s = 2 * duo + k
            unpack(s)
            row = jnp.clip(base[s] - 2 + q, 0, 15)
            v = flat.at[s].reshape(128 * PITCH, 128)[pl.ds(row, 128, stride=PITCH), :]
            if q < 2:
                v = v * low_end[s]
            if q > 9:
                v = v * high_end[s]
            put_row(xbuf.at[duo], q, v, k * lanes)

    def before(op):
        kind, duo, q = op
        if kind == "hidden":
            for r in range(q, q + 3):
                x_row(duo, r)

    def product(op):
        kind, duo, q = op
        if kind == "hidden":
            big, data = big1, window(xbuf.at[duo], q, 3)
        else:
            big, data = big2, window(hbuf.at[duo], q, 4)
        value[op] = jnp.dot(big[...], data, preferred_element_type=F32)

    def after(op):
        kind, duo, q = op
        out = value.pop(op)
        if kind == "hidden":
            hid = out * sigmoid(out)
            for k in range(2):
                v = hid[:, k * lanes : (k + 1) * lanes]
                if q == 0:
                    v = v * low_end[2 * duo + k]
                if q == 9:
                    v = v * high_end[2 * duo + k]
                put_row(hbuf.at[duo], q, v, k * lanes)
            return
        for k in range(2):
            s = 2 * duo + k
            live = jnp.where(s < count, 1.0, 0.0)
            keep = lane >= z0[s]
            for r in range(2):
                part = out[r * 64 : (r + 1) * 64, k * lanes : (k + 1) * lanes]
                weight = jnp.concatenate(
                    [
                        jnp.broadcast_to(
                            gauss_ref[x, pl.ds(base[s] + q + r, 1), :] * live, (16, lanes)
                        )
                        for x in range(4)
                    ],
                    axis=0,
                )
                turned = pltpu.roll(part * weight, lax.rem(z0[s], 128), 1)
                store(mine[s], q + r, jnp.where(keep, turned, 0.0), jnp.where(keep, 0.0, turned))

    order = []
    late = []
    for duo in range(slots // 2):
        for q in range(10):
            order.append(("hidden", duo, q))
            if late:
                order.append(late.pop(0))
        late = [("logits", duo, q) for q in range(0, 8, 2)]
    order += late
    before(order[0])
    before(order[1])
    for i, op in enumerate(order):
        product(op)
        if i > 0:
            after(order[i - 1])
        if i + 2 < len(order):
            before(order[i + 2])
    after(order[-1])


def outer_kernel(
    brick_s,
    z_s,
    count_s,
    feats_hbm,
    gauss_hbm,
    w1_hbm,
    w2_hbm,
    cross_ref,
    total,
    big1,
    big2,
    feats_ref,
    gauss_ref,
    w1_ref,
    w2_ref,
    flat,
    xbuf,
    hbuf,
    sems,
):
    slots = feats_ref.shape[0]
    copies = [
        pltpu.make_async_copy(w1_hbm, w1_ref, sems.at[slots]),
        pltpu.make_async_copy(w2_hbm, w2_ref, sems.at[slots + 1]),
        pltpu.make_async_copy(gauss_hbm, gauss_ref, sems.at[slots + 2]),
    ]
    for copy in copies:
        copy.start()
    loads = [
        pltpu.make_async_copy(feats_hbm.at[s], feats_ref.at[s], sems.at[s]) for s in range(slots)
    ]
    for load in loads:
        load.start()
    total[...] = jnp.zeros_like(total)
    for copy in copies:
        copy.wait()
    for load in loads[:2]:
        load.wait()
    fill_big(big1, band(w1_ref, False), 1)
    fill_big(big2, band(w2_ref, True), 2)

    def store(mine, row, low, high):
        side = jnp.where(mine, 1, 0)
        total[side, row, :, pl.ds(0, 128)] += low
        total[side, row, :, pl.ds(128, 128)] += high

    teacher_half(
        False,
        (brick_s, z_s, count_s),
        lambda s: loads[s].wait() if s >= 2 else None,
        feats_ref,
        gauss_ref,
        big1,
        big2,
        store,
        flat,
        xbuf,
        hbuf,
    )
    cross_ref[...] = total[parity()]


def own_kernel(
    brick_s,
    z_s,
    count_s,
    feats_ref,
    gauss_ref,
    big1,
    big2,
    total,
    main_ref,
    own_ref,
    pair_ref,
    edge_ref,
    flat,
    xbuf,
    hbuf,
):
    own_ref[...] = jnp.zeros_like(own_ref)
    odd = parity()
    pair_ref[...] = total[1 - odd]
    edge_ref[...] = main_ref[pl.ds(6 * (1 - odd), 2)]

    def store(mine, row, low, high):
        own_ref[row, :, pl.ds(0, 128)] += low
        own_ref[row, :, pl.ds(128, 128)] += high

    teacher_half(
        True,
        (brick_s, z_s, count_s),
        lambda s: None,
        feats_ref,
        gauss_ref,
        big1,
        big2,
        store,
        flat,
        xbuf,
        hbuf,
    )


SUMS = jax.ShapeDtypeStruct((8, 64, 256), F32)
EDGE = jax.ShapeDtypeStruct((2, 128, 256), BF16)


def teacher_scratch(slots):
    return [
        pltpu.VMEM((slots, 128, PITCH, 128), F32),
        pltpu.VMEM((slots // 2, 3, 12, 128, 256), BF16),
        pltpu.VMEM((slots // 2, 3, 10, 128, 256), BF16),
    ]


def teacher_outer(brick, z, count, feats, gauss, w1, w2):
    slots = feats.shape[0]
    return pl.pallas_call(
        outer_kernel,
        name="teacher_outer",
        grid_spec=pltpu.PrefetchScalarGridSpec(
            num_scalar_prefetch=3,
            in_specs=[HBM] * 4,
            out_specs=[VMEM] * 6,
            scratch_shapes=[pltpu.VMEM(w1.shape, BF16), pltpu.VMEM(w2.shape, BF16)]
            + teacher_scratch(slots)
            + [pltpu.SemaphoreType.DMA((slots + 3,))],
        ),
        out_shape=[
            SUMS,
            jax.ShapeDtypeStruct((2, 8, 64, 256), F32),
            jax.ShapeDtypeStruct((128, 1152), BF16),
            jax.ShapeDtypeStruct((128, 1536), BF16),
            jax.ShapeDtypeStruct(feats.shape, BF16),
            jax.ShapeDtypeStruct(gauss.shape, F32),
        ],
        compiler_params=params(28),
        cost_estimate=cost(5_000_000_000, 4_000_000),
    )(*map(in_hbm, (brick, z, count, feats, gauss, w1, w2)))


def teacher_own(brick, z, count, feats, gauss, big1, big2, total, main):
    return pl.pallas_call(
        own_kernel,
        name="teacher_own",
        grid_spec=pltpu.PrefetchScalarGridSpec(
            num_scalar_prefetch=3,
            in_specs=[VMEM] * 6,
            out_specs=[VMEM] * 3,
            scratch_shapes=teacher_scratch(feats.shape[0]),
        ),
        out_shape=[SUMS, SUMS, EDGE],
        compiler_params=params(28),
        cost_estimate=cost(4_000_000_000, 3_000_000),
    )(*map(in_hbm, (brick, z, count)), feats, gauss, big1, big2, total, main)


def relay_kernel(feats_hbm, behind, main_ref, cross_ref, feats_ref, flat, sems):
    chunks = 4
    rows = 1024 // chunks
    loads = []
    for i in range(chunks):
        part = pl.ds(i * rows, rows)
        loads.append(pltpu.make_async_copy(feats_hbm.at[part], feats_ref.at[part], sems.at[i]))
        loads[i].start()
    for i in range(chunks):
        loads[i].wait()
        part = pl.ds(i * rows, rows)
        for h in range(2):
            flat[h, part] = feats_ref[part, pl.ds(h * 128, 128)].astype(F32)
            for y in range(8):
                main_ref[y, pl.ds(i * rows // 8, rows // 8), pl.ds(h * 128, 128)] = flat[
                    h, pl.ds(i * rows + y, rows // 8, stride=8), :
                ].astype(BF16)
    cross_ref[...] = main_ref[pl.ds(6 * parity(), 2)]


def relay(feats, behind):
    return pl.pallas_call(
        relay_kernel,
        name="relay",
        in_specs=[HBM, VMEM],
        out_specs=[VMEM] * 2,
        out_shape=[jax.ShapeDtypeStruct((8, 128, 256), BF16), EDGE],
        scratch_shapes=[
            pltpu.VMEM((1024, 256), BF16),
            pltpu.VMEM((2, 1024, 128), F32),
            pltpu.SemaphoreType.DMA((4,)),
        ],
        compiler_params=params(8),
        cost_estimate=cost(0, 1_500_000),
    )(in_hbm(feats), behind)


def put_edges(store, pair_ref, cross_ref, low, high):
    odd = parity()
    for k in range(2):
        pair, cross = pair_ref[k].astype(F32), cross_ref[k].astype(F32)
        store(low + k, jnp.where(odd == 1, pair, cross))
        store(high + k, jnp.where(odd == 1, cross, pair))


def inside(y):
    position = lax.axis_index("gy")
    last = lax.axis_size("gy") - 1
    if y < 0:
        return jnp.where(position > 0, 1.0, 0.0)
    if y >= 8:
        return jnp.where(position < last, 1.0, 0.0)
    return None


def class_softmax(v):
    parts = []
    for x in range(4):
        block = v[x * 16 : (x + 1) * 16]
        peak = jnp.max(block, axis=0, keepdims=True)
        grown = jnp.exp(block - peak)
        parts.append(grown * (1.0 / jnp.sum(grown, axis=0, keepdims=True)))
    return jnp.concatenate(parts, axis=0)


def activate(pre):
    sig = sigmoid(pre)
    return pre * sig, sig * (1.0 + pre * (1.0 - sig))


def two_rows(big_ref, first):
    return jnp.concatenate(
        [big_ref[:, pl.ds((4 * d + first) * 128, 256)] for d in range(3)], axis=1
    )


def forward_kernel(
    main_ref, w1_ref, w2_ref, prob_ref, slope_ref, hbuf, part_ref, big1, big2, back1, back2, xbuf
):
    fill_big(big1, band(w1_ref, False), 2)
    fill_big(big2, band(w2_ref, True), 2)
    for y in range(4):
        put_row(xbuf, y, main_ref[y].astype(F32))
    for y in range(0, 6, 2):
        pre = jnp.dot(big1[...], window(xbuf, y, 4), preferred_element_type=F32)
        if y < 4:
            for k in range(4, 6):
                put_row(xbuf, y + k, main_ref[y + k].astype(F32))
        hid, slope = activate(pre)
        for k in range(2):
            rows = slice(k * 128, (k + 1) * 128)
            slope_ref[y + k] = slope[rows]
            put_row(hbuf, y + k, hid[rows])
    for y in range(0, 4, 2):
        logits = jnp.dot(big2[...], window(hbuf, y, 4), preferred_element_type=F32)
        for k in range(2):
            prob_ref[y + k] = class_softmax(logits[k * 64 : (k + 1) * 64])
    for i, (first, y) in enumerate(((2, 0), (0, 6))):
        part_ref[i] = jnp.dot(
            two_rows(big1, first), window(xbuf, y, 2), preferred_element_type=F32
        )
    flip2 = band(w2_ref, True)
    fill_big(back2, [flip2[8 - t].T for t in range(9)], 2)
    flip1 = band(w1_ref, True)
    fill_big(back1, [flip1[8 - t].T for t in range(9)], 2)


def forward(main, w1, w2):
    return pl.pallas_call(
        forward_kernel,
        name="forward",
        in_specs=[VMEM] * 3,
        out_specs=[VMEM] * 8,
        out_shape=[
            jax.ShapeDtypeStruct((4, 64, 256), F32),
            jax.ShapeDtypeStruct((6, 128, 256), F32),
            jax.ShapeDtypeStruct((3, 6, 128, 256), BF16),
            jax.ShapeDtypeStruct((2, 256, 256), F32),
            jax.ShapeDtypeStruct((256, 1536), BF16),
            jax.ShapeDtypeStruct((128, 1536), BF16),
            jax.ShapeDtypeStruct((256, 1536), BF16),
            jax.ShapeDtypeStruct((256, 768), BF16),
        ],
        scratch_shapes=[pltpu.VMEM((3, 8, 128, 256), BF16)],
        compiler_params=params(16),
        cost_estimate=cost(4_000_000_000, 3_000_000),
    )(main, w1, w2)


def edge_kernel(
    part_ref,
    cross_in,
    pair_in,
    hin_ref,
    big1,
    big2,
    own_ref,
    from_pair_ref,
    from_cross_ref,
    pair_ref,
    cross_ref,
    grad_ref,
    slope_ref,
    xbuf,
    hbuf,
):
    put_edges(lambda y, v: put_row(xbuf, y, v), pair_in, cross_in, 0, 2)
    for d in range(3):
        hbuf[d, pl.ds(2, 2)] = hin_ref[d, pl.ds(0, 2)]
        hbuf[d, pl.ds(4, 2)] = hin_ref[d, pl.ds(4, 2)]
    for g, h, row in ((0, 0, -1), (4, 6, 7)):
        half = g // 2
        pre = part_ref[half // 2] + jnp.dot(
            two_rows(big1, half), window(xbuf, half, 2), preferred_element_type=F32
        )
        hid, slope = activate(pre)
        for k in range(2):
            rows = slice(k * 128, (k + 1) * 128)
            slope_ref[g // 2 + k] = slope[rows]
            keep = inside(row + k)
            put_row(hbuf, h + k, hid[rows] if keep is None else hid[rows] * keep)
    for g, row in ((0, 0), (4, 6)):
        logits = jnp.dot(big2[...], window(hbuf, g, 4), preferred_element_type=F32)
        for k in range(2):
            y = row + k
            value = own_ref[y] + from_pair_ref[y] + from_cross_ref[y]
            prob = class_softmax(logits[k * 64 : (k + 1) * 64])
            grad_ref[g // 2 + k] = (prob - class_softmax(value)).astype(BF16)
    odd = parity()
    pair_ref[...] = grad_ref[pl.ds(2 * (1 - odd), 2)]
    cross_ref[...] = grad_ref[pl.ds(2 * odd, 2)]


def edge_grads(part, cross, pair, hidden, big1, big2, own, from_pair, from_cross):
    edge = jax.ShapeDtypeStruct((2, 64, 256), BF16)
    return pl.pallas_call(
        edge_kernel,
        name="edge_grads",
        in_specs=[VMEM] * 9,
        out_specs=[VMEM] * 4,
        out_shape=[
            edge,
            edge,
            jax.ShapeDtypeStruct((4, 64, 256), BF16),
            jax.ShapeDtypeStruct((4, 128, 256), F32),
        ],
        scratch_shapes=[
            pltpu.VMEM((3, 4, 128, 256), BF16),
            pltpu.VMEM((3, 8, 128, 256), BF16),
        ],
        compiler_params=params(12),
        cost_estimate=cost(2_000_000_000, 3_000_000),
    )(part, cross, pair, hidden, big1, big2, own, from_pair, from_cross)


def put_out(turns, y, grad):
    for k in range(2):
        for x in range(4):
            for h, turn in enumerate(turns):
                at = k * 128 + x * 32
                turn[pl.ds(x * 8 + y + k, 32, stride=32), :] = grad[
                    at : at + 32, h * 128 : (h + 1) * 128
                ]


def inner_kernel(
    own_ref,
    from_pair_ref,
    from_cross_ref,
    prob_ref,
    grad_ref,
    slope_ref,
    big1,
    big2,
    sum_hbm,
    turn0,
    turn1,
    pbuf,
    gbuf,
    sum0,
    sum1,
    sum_ref,
    sem,
):
    for y in range(8):
        value = own_ref[y] + from_pair_ref[y] + from_cross_ref[y]
        for x in range(4):
            for h, turn in enumerate((sum0, sum1)):
                turn[pl.ds(x * 8 + y, 16, stride=32), :] = value[
                    x * 16 : (x + 1) * 16, h * 128 : (h + 1) * 128
                ]
        if 2 <= y < 6:
            grad = (prob_ref[y - 2] - class_softmax(value)).astype(BF16)
        else:
            grad = grad_ref[y if y < 2 else y - 4]
        put_row(gbuf, y, grad.astype(F32))
    sum_ref[:, pl.ds(0, 128)] = sum0[...]
    sum_ref[:, pl.ds(128, 128)] = sum1[...]
    copy = pltpu.make_async_copy(sum_ref, sum_hbm, sem)
    copy.start()
    for y in range(0, 6, 2):
        grad = jnp.dot(big2[...], window(gbuf, y, 4), preferred_element_type=F32)
        for k in range(2):
            put_row(pbuf, y + k, grad[k * 128 : (k + 1) * 128] * slope_ref[y + k])
    for y in range(0, 4, 2):
        grad = jnp.dot(big1[...], window(pbuf, y, 4), preferred_element_type=F32)
        put_out((turn0, turn1), y + 2, grad)
    copy.wait()


def inner(own, from_pair, from_cross, prob, grad, slope, big1, big2):
    turned = jax.ShapeDtypeStruct((1024, 128), F32)
    return pl.pallas_call(
        inner_kernel,
        name="inner",
        in_specs=[VMEM] * 8,
        out_specs=[HBM] + [VMEM] * 3,
        out_shape=[
            jax.ShapeDtypeStruct((512, 256), F32),
            turned,
            turned,
            jax.ShapeDtypeStruct((3, 6, 128, 256), BF16),
        ],
        scratch_shapes=[
            pltpu.VMEM((3, 8, 64, 256), BF16),
            pltpu.VMEM((512, 128), F32),
            pltpu.VMEM((512, 128), F32),
            pltpu.VMEM((512, 256), F32),
            pltpu.SemaphoreType.DMA,
        ],
        compiler_params=params(16),
        cost_estimate=cost(4_000_000_000, 3_000_000),
    )(own, from_pair, from_cross, prob, grad, slope, big1, big2)


def outer_rows_kernel(
    main_ref,
    cross_ref,
    pair_ref,
    slope_ref,
    done0,
    done1,
    pin_ref,
    big1,
    big2,
    out_hbm,
    gbuf,
    pbuf,
    turn0,
    turn1,
    out_ref,
    sems,
):
    store = lambda y, v: put_row(gbuf, y, v)
    put_edges(store, pair_ref, cross_ref, 0, 6)
    for y in range(4):
        store(y + 2, main_ref[y].astype(F32))
    for d in range(3):
        pbuf[d, pl.ds(2, 2)] = pin_ref[d, pl.ds(0, 2)]
        pbuf[d, pl.ds(4, 2)] = pin_ref[d, pl.ds(4, 2)]
    for g, p, row in ((0, 0, -1), (4, 6, 7)):
        grad = jnp.dot(big2[...], window(gbuf, g, 4), preferred_element_type=F32)
        for k in range(2):
            v = grad[k * 128 : (k + 1) * 128] * slope_ref[g // 2 + k]
            keep = inside(row + k)
            put_row(pbuf, p + k, v if keep is None else v * keep)
    y = lax.broadcasted_iota(jnp.int32, (32, 16, 128), 1) % 8
    early = (y >= 2) & (y < 6)
    copies = []
    for i in range(2):
        half = jnp.concatenate([big1[pl.ds(k * 128 + i * 64, 64)] for k in range(2)], axis=0)
        for p, row in ((0, 0), (4, 6)):
            grad = jnp.dot(half, window(pbuf, p, 4), preferred_element_type=F32)
            for k in range(2):
                for x in range(2):
                    for h, turn in enumerate((turn0, turn1)):
                        at = k * 64 + x * 32
                        turn[pl.ds((2 * i + x) * 8 + row + k, 32, stride=32), :] = grad[
                            at : at + 32, h * 128 : (h + 1) * 128
                        ]
        part = pl.ds(i * 16, 16)
        for h, (turn, done) in enumerate(((turn0, done0), (turn1, done1))):
            late = turn.reshape(32, 32, 128)[:, part]
            kept = done.reshape(32, 32, 128)[:, part]
            out_ref[i, :, :, pl.ds(h * 128, 128)] = jnp.where(early, kept, late)
        copies.append(pltpu.make_async_copy(out_ref.at[i], out_hbm.at[:, part], sems.at[i]))
        copies[i].start()
    for copy in copies:
        copy.wait()


def outer_rows(main, cross, pair, slope, done0, done1, pin, big1, big2):
    return pl.pallas_call(
        outer_rows_kernel,
        name="outer_rows",
        in_specs=[VMEM] * 9,
        out_specs=HBM,
        out_shape=jax.ShapeDtypeStruct((32, 32, 256), F32),
        scratch_shapes=[
            pltpu.VMEM((3, 8, 64, 256), BF16),
            pltpu.VMEM((3, 8, 128, 256), BF16),
            pltpu.VMEM((1024, 128), F32),
            pltpu.VMEM((1024, 128), F32),
            pltpu.VMEM((2, 32, 16, 256), F32),
            pltpu.SemaphoreType.DMA((2,)),
        ],
        compiler_params=params(16),
        cost_estimate=cost(2_000_000_000, 3_000_000),
    )(main, cross, pair, slope, done0, done1, pin, big1, big2)


def swap_pair(value):
    count = lax.axis_size("gy")
    return lax.ppermute(value, "gy", [(i, i ^ 1) for i in range(count)])


def swap_cross(value):
    count = lax.axis_size("gy")
    pairs = [(i, i + 1) for i in range(1, count - 1, 2)]
    return lax.ppermute(value, "gy", pairs + [(j, i) for i, j in pairs])


def taps_first(w):
    outs, ins = w.shape[:2]
    return jnp.transpose(w, (2, 3, 4, 0, 1)).reshape(3, 9, outs, ins)


def body(
    window_feats,
    window_brick,
    window_z,
    window_count,
    gaussian,
    brick_feats,
    teacher_w1,
    teacher_w2,
    student_w1,
    student_w2,
):
    tw1, tw2, sw1, sw2 = map(taps_first, (teacher_w1, teacher_w2, student_w1, student_w2))
    feats = window_feats.reshape(window_feats.shape[0], 2048, 128)
    tables = (window_brick, window_z, window_count)
    sum_cross, sides, big1, big2, held_feats, held_gauss = teacher_outer(
        *tables, feats, gaussian, tw1, tw2
    )
    got_cross = swap_cross(sum_cross)
    main, to_cross = relay(brick_feats.reshape(1024, 256), held_gauss)
    edge_cross = swap_cross(to_cross)
    own, sum_pair, to_pair = teacher_own(
        *tables, held_feats, held_gauss, big1, big2, sides, main
    )
    got_pair = swap_pair(sum_pair)
    edge_pair = swap_pair(to_pair)
    prob, slope, hidden, part, near1, near2, back1, back2 = forward(main, sw1, sw2)
    sums = (own, got_pair, got_cross)
    grad_pair, grad_cross, grad, slope_ends = edge_grads(
        part, edge_cross, edge_pair, hidden, near1, near2, *sums
    )
    near_pair = swap_pair(grad_pair)
    near_cross = swap_cross(grad_cross)
    teacher_sum, *early = inner(*sums, prob, grad, slope, back1, back2)
    feature_grad = outer_rows(grad, near_cross, near_pair, slope_ends, *early, back1, back2)
    return (teacher_sum.reshape(16, 4, 8, 256), feature_grad.reshape(32, 4, 8, 256))


def solution(mesh):
    placed = (
        P(("grp", "gy"), None, None, None, None),
        P("grp"),
        P("grp"),
        P("grp"),
        P(),
        P(None, None, ("grp", "gy"), None),
        P(),
        P(),
        P(),
        P(),
    )
    return jax.shard_map(
        body,
        mesh=mesh,
        in_specs=placed,
        out_specs=(P(None, None, ("grp", "gy"), None), P(None, None, ("grp", "gy"), None)),
        check_vma=False,
    )
```
